128 devices in a mesh: win: 4 (over z_lo, core), lat: 32 (over y, z_hi, x).
Axes of the slice: x: 4, y: 4, z: 4 (z_hi: 2, z_lo: 2; z = z_hi * 2 + z_lo), core: 2. Of those that a mesh axis runs over, the one named last changes fastest.
Arguments:
- increments: float32 [16, 1024, 8, 1024], P('win', 'lat'), may hold values from -6 to 6
- courant_lon: float32 [1024, 8, 1024], P('lat'), may hold values from -0.5 to 0.5
- courant_lat: float32 [1024, 8, 1024], P('lat'), may hold values from -0.5 to 0.5
- lat_factor: float32 [1024, 1024], replicated, may hold values from -0.1875 to 0.1875
- lon_factor: float32 [1024, 1024], replicated, may hold values from -0.1875 to 0.1875
Outputs:
- updated: float32 [16, 1024, 8, 1024], P('win', 'lat')
The draws below stay inside these ranges and needn't reach their ends.
All inputs are finite; a program needn't handle non-finite values.
Results may differ from the reference program's by a relative error of at most 0.00005.
Values sent between devices are 32-bit elements; how exact they have to be, the bound alone decides.
A program may use at most 192 MiB of HBM per device.

```python
import math
import jax
import jax.numpy as jnp
from jax import lax

STEPS = 4
LEVELS = 8
NLON = 1024
SUBW = 16
NLAT = 1024


def shard_levels(own_key, shape, cuts, smallest, largest):
    def one(dim, blocks):
        heights = jax.random.uniform(jax.random.fold_in(jax.random.fold_in(own_key, 6), dim), (blocks,), jnp.float32, smallest / len(cuts), largest / len(cuts))
        return jnp.repeat(jnp.exp(heights), shape[dim] // blocks).reshape((-1,) + (1,) * (len(shape) - dim - 1))

    loudness = one(*cuts[0])
    for cut in cuts[1:]:
        loudness = loudness * one(*cut)
    return loudness


def noise(stream_key, dims, spread, bound, shards=(), kind=jnp.bfloat16):
    drawn = jax.random.normal(stream_key, dims, jnp.float32) * spread
    if len(shards) > 0:
        drawn = shard_levels(stream_key, dims, shards, -0.22, 0.18) * drawn
    return jnp.clip(drawn, min=-bound, max=bound).astype(kind)


def setup_inputs(seed: int = 0) -> dict:
    key_list = jax.random.split(jax.random.key(seed), 6)
    increments = noise(key_list[0], (SUBW, NLAT, LEVELS, NLON), 1.0, 6.0, ((0, 4), (1, 32)), jnp.float32)
    courant_lon = jnp.clip(jax.random.uniform(key_list[1], (NLAT, LEVELS, NLON), jnp.float32, -0.5, 0.5) * shard_levels(key_list[1], (NLAT, LEVELS, NLON), ((0, 32),), -0.4, 0.0), -0.5, 0.5)
    courant_lat = jnp.clip(jax.random.uniform(key_list[2], (NLAT, LEVELS, NLON), jnp.float32, -0.5, 0.5) * shard_levels(key_list[2], (NLAT, LEVELS, NLON), ((0, 32),), -0.4, 0.0), -0.5, 0.5)
    lat_factor = noise(key_list[3], (NLAT, NLAT), NLAT ** -0.5, 0.1875, (), jnp.float32)
    lon_factor = noise(key_list[4], (NLON, NLON), NLON ** -0.5, 0.1875, (), jnp.float32)
    return dict(increments=increments, courant_lon=courant_lon, courant_lat=courant_lat, lat_factor=lat_factor, lon_factor=lon_factor)


diffusion = 0.125
turning_scale = 0.6


def advance(extended, lon_speed, lat_speed, cosine_row, sine_row):
    middle = extended[1:-1]
    east = jnp.roll(middle, -1, axis=2)
    west = jnp.roll(middle, 1, axis=2)
    lat_diff = extended[2:] - extended[:-2]
    lon_diff = east - west
    laplace = east + west + extended[2:] + extended[:-2] - 4.0 * middle
    moved = middle - 0.5 * lon_speed * lon_diff - 0.5 * lat_speed * lat_diff + diffusion * laplace
    row_count, levels, columns = moved.shape
    paired = moved.reshape(row_count, levels // 2, 2, columns)
    first_lev = paired[:, :, 0]
    second_lev = paired[:, :, 1]
    cosine_b = cosine_row[:, None, None]
    sine_b = sine_row[:, None, None]
    turned = jnp.stack([cosine_b * first_lev + sine_b * second_lev, cosine_b * second_lev - sine_b * first_lev], axis=2)
    return turned.reshape(row_count, levels, columns)


def reference(increments, courant_lon, courant_lat, lat_factor, lon_factor):
    row_ids = jnp.arange(NLAT, dtype=jnp.float32)
    theta = turning_scale * jnp.cos(math.pi * (row_ids + 0.5) / NLAT)
    cosine_row = jnp.cos(theta)
    sine_row = jnp.sin(theta)

    def integrate(field):
        for step_index in range(STEPS):
            extended = jnp.pad(field, ((1, 1), (0, 0), (0, 0)))
            field = advance(extended, courant_lon, courant_lat, cosine_row, sine_row)
        return field

    end_states = lax.map(integrate, increments)
    previous = jnp.concatenate([jnp.zeros_like(end_states[:1]), end_states[:-1]], axis=0)
    defects = increments - previous
    field_shape = defects.shape
    along = jnp.dot(defects.reshape(-1, NLON), lon_factor, precision=lax.Precision.HIGHEST).reshape(field_shape)

    def mix_rows(block):
        return jnp.einsum('ik,klm->ilm', lat_factor, block, precision=lax.Precision.HIGHEST)

    applied = lax.map(mix_rows, along)
    return increments - 0.5 * applied
```

```python
import math

import jax
import jax.numpy as jnp
from jax import lax
from jax.experimental import pallas as pl
from jax.experimental.pallas import tpu as pltpu
from jax.sharding import PartitionSpec as P

STEPS = 4
WINS = 4
ROWS = 32
LEVELS = 8
NLON = 1024
NLAT = 1024
LATS = 32
EXT = ROWS + 2 * STEPS
COLS = 256
TILES = NLON // 128
MESH = pl.DeviceIdType.MESH

diffusion = 0.125
turning_scale = 0.6

f32 = jnp.float32
bf16 = jnp.bfloat16


def split(value):
    high = value.astype(bf16)
    low = (value - high.astype(f32)).astype(bf16)
    return high, low


def dot(a, b):
    return jnp.dot(a, b, preferred_element_type=f32)


def kernel(
    inc, clon, clat, lat_fac, lon_fac,
    out,
    field, cl, ca, cos_t, sin_t, t1, t2,
    stage, lhi, llo, rhi, rlo,
    ends, arrived, work, mixed, ahi, alo, xhi, xlo,
    send, recv, back, ret,
    load_sem, stage_sem, hs_sem, hr_sem, es_sem, er_sem,
    fs_sem, fr_sem, bs_sem, br_sem, out_sem,
):
    lat = lax.axis_index("lat")
    win = lax.axis_index("win")
    other = lax.rem(win + 2, 4)
    north = lax.rem(lat + LATS - 1, LATS)
    south = lax.rem(lat + 1, LATS)
    nxt = lax.rem(win + 1, 4)
    prv = lax.rem(win + 3, 4)

    loads = []
    for w in range(WINS):
        loads.append(
            pltpu.make_async_copy(inc.at[w], field.at[w, pl.ds(STEPS, ROWS)], load_sem.at[w])
        )
    loads.append(pltpu.make_async_copy(clon, cl.at[pl.ds(STEPS, ROWS)], load_sem.at[4]))
    loads.append(pltpu.make_async_copy(clat, ca.at[pl.ds(STEPS, ROWS)], load_sem.at[5]))
    for copy in (loads[4], loads[5], loads[0], loads[1], loads[2], loads[3]):
        copy.start()
    factor_loads = [
        pltpu.make_async_copy(lon_fac, stage.at[0], stage_sem.at[0]),
        pltpu.make_async_copy(lat_fac, stage.at[1], stage_sem.at[1]),
    ]
    for copy in factor_loads:
        copy.start()

    barrier = pltpu.get_barrier_semaphore()

    def greet(k, carry):
        pl.semaphore_signal(
            barrier, inc=1, device_id=(other, lax.rem(lat + k, LATS)), device_id_type=MESH
        )
        return carry

    for where in ((win, north), (win, south), (nxt, lat), (prv, lat)):
        pl.semaphore_signal(barrier, inc=1, device_id=where, device_id_type=MESH)
    lax.fori_loop(0, LATS, greet, 0)

    row = lax.broadcasted_iota(jnp.int32, (EXT, LEVELS, 128), 0) + (lat * ROWS - STEPS)
    inside = ((row >= 0) & (row < NLAT)).astype(f32)
    theta = turning_scale * jnp.cos(math.pi * (row.astype(f32) + 0.5) / NLAT)
    even3 = lax.rem(lax.broadcasted_iota(jnp.int32, (EXT, LEVELS, 128), 1), 2) == 0
    cos_t[...] = 0.5 * jnp.cos(theta) * inside
    sin_half = 0.5 * jnp.sin(theta) * inside
    sin_t[...] = jnp.where(even3, sin_half, -sin_half)

    pl.semaphore_wait(barrier, LATS + 4)

    halos = []

    def halo(src, dst, slot, where):
        copy = pltpu.make_async_remote_copy(
            src_ref=src, dst_ref=dst, send_sem=hs_sem.at[slot], recv_sem=hr_sem.at[slot],
            device_id=(win, where), device_id_type=MESH,
        )
        copy.start()
        halos.append(copy)

    def window_halo(w):
        halo(inc.at[w, pl.ds(ROWS - STEPS, STEPS)], field.at[w, pl.ds(0, STEPS)], 2 * w, south)
        halo(inc.at[w, pl.ds(0, STEPS)], field.at[w, pl.ds(STEPS + ROWS, STEPS)], 2 * w + 1, north)

    EDGE = STEPS - 1
    window_halo(0)
    halo(clon.at[pl.ds(ROWS - EDGE, EDGE)], cl.at[pl.ds(1, EDGE)], 8, south)
    halo(clon.at[pl.ds(0, EDGE)], cl.at[pl.ds(STEPS + ROWS, EDGE)], 9, north)
    halo(clat.at[pl.ds(ROWS - EDGE, EDGE)], ca.at[pl.ds(1, EDGE)], 10, south)
    halo(clat.at[pl.ds(0, EDGE)], ca.at[pl.ds(STEPS + ROWS, EDGE)], 11, north)
    window_halo(3)
    window_halo(1)
    window_halo(2)
    halo_of = {0: halos[0:2], 3: halos[6:8], 1: halos[8:10], 2: halos[10:12]}
    courant_halos = halos[2:6]

    def split_into(slot, high_ref, low_ref):
        def some(k, carry):
            rows = pl.ds(pl.multiple_of(k * 32, 32), 32)
            high, low = split(stage[slot, rows, :])
            high_ref[rows, :] = high
            low_ref[rows, :] = low
            return carry

        factor_loads[slot].wait()
        lax.fori_loop(0, NLAT // 32, some, 0)

    split_into(0, rhi, rlo)
    split_into(1, lhi, llo)

    loads[4].wait()
    loads[5].wait()
    for copy in courant_halos:
        copy.wait_recv()

    def coefficients(r, carry):
        cl[r] = 0.25 - cl[r]
        ca[r] = 0.25 - ca[r]
        return carry

    lax.fori_loop(1, EXT - 1, coefficients, 0, unroll=2)

    even = lax.rem(lax.broadcasted_iota(jnp.int32, (LEVELS, NLON), 0), 2) == 0

    def one_row(src, r):
        n = src[r - 1]
        c = src[r]
        s = src[r + 1]
        e = pltpu.roll(c, NLON - 1, 1)
        w = pltpu.roll(c, 1, 1)
        y = (c + 0.5 * (w + n)) + cl[r] * (e - w) + ca[r] * (s - n)
        swapped = jnp.where(even, pltpu.roll(y, LEVELS - 1, 0), pltpu.roll(y, 1, 0))
        cosine = jnp.concatenate([cos_t[r]] * (NLON // 128), axis=1)
        sine = jnp.concatenate([sin_t[r]] * (NLON // 128), axis=1)
        return cosine * y + sine * swapped

    def advance(src, dst, first, last):
        def rows(r, carry):
            dst[r] = one_row(src, r)
            return carry

        lax.fori_loop(first, last, rows, 0, unroll=2)

    def integrate(w, finish):
        for copy in halo_of[w]:
            copy.wait_recv()
        source = field.at[w]

        @pl.when(lat == 0)
        def _():
            source[0:STEPS] = jnp.zeros((STEPS, LEVELS, NLON), f32)

        @pl.when(lat == LATS - 1)
        def _():
            source[STEPS + ROWS : EXT] = jnp.zeros((STEPS, LEVELS, NLON), f32)

        advance(source, t1, 1, EXT - 1)
        advance(t1, t2, 2, EXT - 2)
        advance(t2, t1, 3, EXT - 3)

        def last(r, carry):
            finish(r, one_row(t1, r + STEPS))
            return carry

        lax.fori_loop(0, ROWS, last, 0, unroll=2)

    def put_row(r, value):
        for t in range(TILES):
            work[t, pl.ds(pl.multiple_of(r * LEVELS, LEVELS), LEVELS), :] = value[
                :, t * 128 : (t + 1) * 128
            ]

    def level_rows(level):
        return pl.ds(level, ROWS, stride=LEVELS)

    def to_defect(w):
        def finish(r, value):
            put_row(r, field[w, r + STEPS] - value)

        return finish

    def to_ends(r, value):
        ends[r] = value

    def along_lon():
        def block(k, carry):
            cols = pl.ds(pl.multiple_of(k * 256, 256), 256)
            right = rhi[:, cols]
            both = dot(ahi[...], right) + dot(alo[...], right) + dot(ahi[...], rlo[:, cols])
            mixed[2 * k] = both[:, :128]
            mixed[2 * k + 1] = both[:, 128:]
            return carry

        lax.fori_loop(0, NLON // 256, block, 0)

    def split_work():
        for t in range(TILES):
            high, low = split(work[t])
            ahi[:, t * 128 : (t + 1) * 128] = high
            alo[:, t * 128 : (t + 1) * 128] = low

    def send_forward(w, source):
        for level in range(LEVELS):
            for t in range(TILES):
                send[w, level * 4 + t // 2, :, (t % 2) * 128 : (t % 2 + 1) * 128] = source[
                    t, level_rows(level), :
                ]

        def go(k, carry):
            j = lax.rem(lat + k, LATS)
            pltpu.make_async_remote_copy(
                src_ref=send.at[w, j],
                dst_ref=recv.at[w, pl.ds(pl.multiple_of(lat * ROWS, ROWS), ROWS)],
                send_sem=fs_sem.at[w], recv_sem=fr_sem.at[w],
                device_id=(other, j), device_id_type=MESH,
            ).start()
            return carry

        lax.fori_loop(0, LATS, go, 0)

    def mix(w):
        pltpu.make_async_copy(recv.at[w], recv.at[w], fr_sem.at[w]).wait()

        def some(k, carry):
            rows = pl.ds(pl.multiple_of(k * 128, 128), 128)
            high, low = split(recv[w, rows, :])
            xhi[rows, :] = high
            xlo[rows, :] = low
            return carry

        lax.fori_loop(0, NLAT // 128, some, 0)

        def block(k, carry):
            first = lax.rem(lat // 8 + k, 4)
            rows = pl.ds(pl.multiple_of(first * 256, 256), 256)
            left = lhi[rows, :]
            back[w, rows, :] = (
                dot(left, xhi[...]) + dot(left, xlo[...]) + dot(llo[rows, :], xhi[...])
            )

            def go(i, inner):
                j = first * 8 + lax.rem(lat + i, 8)
                pltpu.make_async_remote_copy(
                    src_ref=back.at[w, pl.ds(pl.multiple_of(j * ROWS, ROWS), ROWS)],
                    dst_ref=ret.at[w, lat],
                    send_sem=bs_sem.at[w], recv_sem=br_sem.at[w],
                    device_id=(other, j), device_id_type=MESH,
                ).start()
                return inner

            lax.fori_loop(0, 8, go, 0)
            return carry

        lax.fori_loop(0, 4, block, 0)

    def finish_window(w, lon_done):
        pltpu.make_async_copy(ret.at[w], ret.at[w], br_sem.at[w]).wait()
        if lon_done:
            for level in range(LEVELS):
                for t in range(TILES):
                    work[t, level_rows(level), :] = ret[
                        w, level * 4 + t // 2, :, (t % 2) * 128 : (t % 2 + 1) * 128
                    ]
        else:
            for level in range(LEVELS):
                for quarter in range(4):
                    high, low = split(ret[w, level * 4 + quarter])
                    rows = slice(level * ROWS, (level + 1) * ROWS)
                    cols = slice(quarter * COLS, (quarter + 1) * COLS)
                    ahi[rows, cols] = high
                    alo[rows, cols] = low
            along_lon()
            for level in range(LEVELS):
                for t in range(TILES):
                    work[t, level_rows(level), :] = mixed[t, level * ROWS : (level + 1) * ROWS, :]

        def update(r, carry):
            rows = pl.ds(pl.multiple_of(r * LEVELS, LEVELS), LEVELS)
            applied = jnp.concatenate([work[t, rows, :] for t in range(TILES)], axis=1)
            field[w, r + STEPS] = field[w, r + STEPS] - 0.5 * applied
            return carry

        lax.fori_loop(0, ROWS, update, 0, unroll=2)
        pltpu.make_async_copy(
            field.at[w, pl.ds(STEPS, ROWS)], out.at[w], out_sem.at[w]
        ).start()

    loads[0].wait()
    loads[1].wait()
    integrate(0, to_defect(1))
    send_forward(1, work)

    loads[3].wait()
    integrate(3, to_ends)
    ends_copy = pltpu.make_async_remote_copy(
        src_ref=ends, dst_ref=arrived, send_sem=es_sem, recv_sem=er_sem,
        device_id=(nxt, lat), device_id_type=MESH,
    )

    @pl.when(win < 3)
    def _():
        ends_copy.start()

    loads[2].wait()
    integrate(1, to_defect(2))
    split_work()
    along_lon()
    send_forward(2, mixed)

    mix(1)

    integrate(2, to_defect(3))
    split_work()
    along_lon()
    send_forward(3, mixed)

    @pl.when(win > 0)
    def _():
        ends_copy.wait_recv()

    @pl.when(win == 0)
    def _():
        arrived[...] = jnp.zeros_like(arrived)

    def first_defect(r, carry):
        put_row(r, field[0, r + STEPS] - arrived[r])
        return carry

    lax.fori_loop(0, ROWS, first_defect, 0, unroll=2)
    split_work()
    along_lon()
    send_forward(0, mixed)

    mix(2)
    finish_window(1, False)
    mix(3)
    finish_window(2, True)
    mix(0)
    finish_window(3, True)
    finish_window(0, True)

    for copy in halos:
        copy.wait_send()

    @pl.when(win < 3)
    def _():
        ends_copy.wait_send()

    for w in range(WINS):
        pltpu.make_async_copy(send.at[w], send.at[w], fs_sem.at[w]).wait()
        pltpu.make_async_copy(back.at[w], back.at[w], bs_sem.at[w]).wait()
        pltpu.make_async_copy(field.at[w, pl.ds(STEPS, ROWS)], out.at[w], out_sem.at[w]).wait()


def shards(increments, courant_lon, courant_lat, lat_factor, lon_factor):
    any_space = pl.BlockSpec(memory_space=pl.ANY)
    strip = (EXT, LEVELS, NLON)
    dma = pltpu.SemaphoreType.DMA
    return pl.pallas_call(
        kernel,
        out_shape=jax.ShapeDtypeStruct((WINS, ROWS, LEVELS, NLON), f32),
        in_specs=[any_space] * 5,
        out_specs=any_space,
        scratch_shapes=[
            pltpu.VMEM((WINS,) + strip, f32),
            pltpu.VMEM(strip, f32),
            pltpu.VMEM(strip, f32),
            pltpu.VMEM((EXT, LEVELS, 128), f32),
            pltpu.VMEM((EXT, LEVELS, 128), f32),
            pltpu.VMEM(strip, f32),
            pltpu.VMEM(strip, f32),
            pltpu.VMEM((2, NLAT, NLON), f32),
            pltpu.VMEM((NLAT, NLAT), bf16),
            pltpu.VMEM((NLAT, NLAT), bf16),
            pltpu.VMEM((NLON, NLON), bf16),
            pltpu.VMEM((NLON, NLON), bf16),
            pltpu.VMEM((ROWS, LEVELS, NLON), f32),
            pltpu.VMEM((ROWS, LEVELS, NLON), f32),
            pltpu.VMEM((TILES, ROWS * LEVELS, 128), f32),
            pltpu.VMEM((TILES, ROWS * LEVELS, 128), f32),
            pltpu.VMEM((ROWS * LEVELS, NLON), bf16),
            pltpu.VMEM((ROWS * LEVELS, NLON), bf16),
            pltpu.VMEM((NLAT, COLS), bf16),
            pltpu.VMEM((NLAT, COLS), bf16),
            pltpu.VMEM((WINS, LATS, ROWS, COLS), f32),
            pltpu.VMEM((WINS, NLAT, COLS), f32),
            pltpu.VMEM((WINS, NLAT, COLS), f32),
            pltpu.VMEM((WINS, LATS, ROWS, COLS), f32),
            dma((6,)),
            dma((2,)),
            dma((12,)),
            dma((12,)),
            dma,
            dma,
            dma((WINS,)),
            dma((WINS,)),
            dma((WINS,)),
            dma((WINS,)),
            dma((WINS,)),
        ],
        compiler_params=pltpu.CompilerParams(
            collective_id=0, has_side_effects=True, vmem_limit_bytes=60 << 20
        ),
        name="subwindows",
    )(increments, courant_lon, courant_lat, lat_factor, lon_factor)


def solution(mesh):
    in_specs = (P("win", "lat", None, None), P("lat", None, None), P("lat", None, None), P(), P())
    out_specs = P("win", "lat", None, None)
    return jax.shard_map(shards, mesh=mesh, in_specs=in_specs, out_specs=out_specs, check_vma=False)
```

```python
import math

import jax
import jax.numpy as jnp
from jax import lax
from jax.experimental import pallas as pl
from jax.experimental.pallas import tpu as pltpu
from jax.sharding import PartitionSpec as P

STEPS = 4
WINS = 4
ROWS = 32
LEVELS = 8
NLON = 1024
NLAT = 1024
LATS = 32
EXT = ROWS + 2 * STEPS
COLS = 256
TILES = NLON // 128
MESH = pl.DeviceIdType.MESH

diffusion = 0.125
turning_scale = 0.6

f32 = jnp.float32
bf16 = jnp.bfloat16


def split(value):
    high = value.astype(bf16)
    low = (value - high.astype(f32)).astype(bf16)
    return high, low


def dot(a, b):
    return jnp.dot(a, b, preferred_element_type=f32)


def kernel(
    inc, clon, clat, lat_fac, lon_fac,
    out,
    field, cl, ca, cos_t, sin_t, t1, t2,
    stage, lhi, llo, rhi, rlo,
    ends, arrived, work, mixed, ahi, alo, xhi, xlo,
    send, recv, back, ret,
    load_sem, stage_sem, hs_sem, hr_sem, es_sem, er_sem,
    fs_sem, fr_sem, bs_sem, br_sem, out_sem,
):
    lat = lax.axis_index("lat")
    win = lax.axis_index("win")
    other = lax.rem(win + 2, 4)
    north = lax.rem(lat + LATS - 1, LATS)
    south = lax.rem(lat + 1, LATS)
    nxt = lax.rem(win + 1, 4)
    prv = lax.rem(win + 3, 4)

    loads = []
    for w in range(WINS):
        loads.append(
            pltpu.make_async_copy(inc.at[w], field.at[w, pl.ds(STEPS, ROWS)], load_sem.at[w])
        )
    loads.append(pltpu.make_async_copy(clon, cl.at[pl.ds(STEPS, ROWS)], load_sem.at[4]))
    loads.append(pltpu.make_async_copy(clat, ca.at[pl.ds(STEPS, ROWS)], load_sem.at[5]))
    for copy in (loads[4], loads[5], loads[0], loads[1], loads[2], loads[3]):
        copy.start()
    factor_loads = [
        pltpu.make_async_copy(lon_fac, stage.at[0], stage_sem.at[0]),
        pltpu.make_async_copy(lat_fac, stage.at[1], stage_sem.at[1]),
    ]
    for copy in factor_loads:
        copy.start()

    barrier = pltpu.get_barrier_semaphore()

    def greet(k, carry):
        pl.semaphore_signal(
            barrier, inc=1, device_id=(other, lax.rem(lat + k, LATS)), device_id_type=MESH
        )
        return carry

    for where in ((win, north), (win, south), (nxt, lat), (prv, lat)):
        pl.semaphore_signal(barrier, inc=1, device_id=where, device_id_type=MESH)
    lax.fori_loop(0, LATS, greet, 0)

    row = lax.broadcasted_iota(jnp.int32, (EXT, LEVELS, 128), 0) + (lat * ROWS - STEPS)
    inside = ((row >= 0) & (row < NLAT)).astype(f32)
    theta = turning_scale * jnp.cos(math.pi * (row.astype(f32) + 0.5) / NLAT)
    even3 = lax.rem(lax.broadcasted_iota(jnp.int32, (EXT, LEVELS, 128), 1), 2) == 0
    cos_t[...] = 0.5 * jnp.cos(theta) * inside
    sin_half = 0.5 * jnp.sin(theta) * inside
    sin_t[...] = jnp.where(even3, sin_half, -sin_half)

    pl.semaphore_wait(barrier, LATS + 4)

    halos = []

    def halo(src, dst, slot, where):
        copy = pltpu.make_async_remote_copy(
            src_ref=src, dst_ref=dst, send_sem=hs_sem.at[slot], recv_sem=hr_sem.at[slot],
            device_id=(win, where), device_id_type=MESH,
        )
        copy.start()
        halos.append(copy)

    def window_halo(w):
        halo(inc.at[w, pl.ds(ROWS - STEPS, STEPS)], field.at[w, pl.ds(0, STEPS)], 2 * w, south)
        halo(inc.at[w, pl.ds(0, STEPS)], field.at[w, pl.ds(STEPS + ROWS, STEPS)], 2 * w + 1, north)

    EDGE = STEPS - 1
    window_halo(0)
    halo(clon.at[pl.ds(ROWS - EDGE, EDGE)], cl.at[pl.ds(1, EDGE)], 8, south)
    halo(clon.at[pl.ds(0, EDGE)], cl.at[pl.ds(STEPS + ROWS, EDGE)], 9, north)
    halo(clat.at[pl.ds(ROWS - EDGE, EDGE)], ca.at[pl.ds(1, EDGE)], 10, south)
    halo(clat.at[pl.ds(0, EDGE)], ca.at[pl.ds(STEPS + ROWS, EDGE)], 11, north)

    def split_into(slot, high_ref, low_ref):
        def some(k, carry):
            rows = pl.ds(pl.multiple_of(k * 32, 32), 32)
            high, low = split(stage[slot, rows, :])
            high_ref[rows, :] = high
            low_ref[rows, :] = low
            return carry

        factor_loads[slot].wait()
        lax.fori_loop(0, NLAT // 32, some, 0)

    def coefficients(first, last):
        def some(r, carry):
            cl[r] = 0.25 - cl[r]
            ca[r] = 0.25 - ca[r]
            return carry

        lax.fori_loop(first, last, some, 0, unroll=True if last - first < 8 else 2)

    loads[4].wait()
    loads[5].wait()
    coefficients(STEPS, STEPS + ROWS)

    even = lax.rem(lax.broadcasted_iota(jnp.int32, (LEVELS, NLON), 0), 2) == 0

    def one_row(src, r):
        n = src[r - 1]
        c = src[r]
        s = src[r + 1]
        e = pltpu.roll(c, NLON - 1, 1)
        w = pltpu.roll(c, 1, 1)
        y = (c + 0.5 * (w + n)) + cl[r] * (e - w) + ca[r] * (s - n)
        swapped = jnp.where(even, pltpu.roll(y, LEVELS - 1, 0), pltpu.roll(y, 1, 0))
        cosine = jnp.concatenate([cos_t[r]] * (NLON // 128), axis=1)
        sine = jnp.concatenate([sin_t[r]] * (NLON // 128), axis=1)
        return cosine * y + sine * swapped

    def advance(src, dst, first, last):
        def rows(r, carry):
            dst[r] = one_row(src, r)
            return carry

        lax.fori_loop(first, last, rows, 0, unroll=2)

    def last_step(first, last, finish):
        def some(r, carry):
            finish(r, one_row(t1, r + STEPS))
            return carry

        lax.fori_loop(first, last, some, 0, unroll=2)

    def outside_is_zero(w):
        @pl.when(lat == 0)
        def _():
            field[w, 0:STEPS] = jnp.zeros((STEPS, LEVELS, NLON), f32)

        @pl.when(lat == LATS - 1)
        def _():
            field[w, STEPS + ROWS : EXT] = jnp.zeros((STEPS, LEVELS, NLON), f32)

    def integrate(w, finish):
        for copy in halo_of[w]:
            copy.wait_recv()
        outside_is_zero(w)
        advance(field.at[w], t1, 1, EXT - 1)
        advance(t1, t2, 2, EXT - 2)
        advance(t2, t1, 3, EXT - 3)
        last_step(0, ROWS, finish)

    def interior(w, finish):
        advance(field.at[w], t1, 5, EXT - 5)
        advance(t1, t2, 6, EXT - 6)
        advance(t2, t1, 7, EXT - 7)
        last_step(STEPS, ROWS - STEPS, finish)

    def edges(w, finish):
        outside_is_zero(w)
        for src, dst, step in ((field.at[w], t1, 1), (t1, t2, 2), (t2, t1, 3)):
            advance(src, dst, step, step + 4)
            advance(src, dst, EXT - step - 4, EXT - step)
        last_step(0, STEPS, finish)
        last_step(ROWS - STEPS, ROWS, finish)

    def put_row(r, value):
        for t in range(TILES):
            work[t, pl.ds(pl.multiple_of(r * LEVELS, LEVELS), LEVELS), :] = value[
                :, t * 128 : (t + 1) * 128
            ]

    def level_rows(level):
        return pl.ds(level, ROWS, stride=LEVELS)

    def to_defect(w):
        def finish(r, value):
            put_row(r, field[w, r + STEPS] - value)

        return finish

    def to_ends(r, value):
        ends[r] = value

    def along_lon():
        def block(k, carry):
            cols = pl.ds(pl.multiple_of(k * 256, 256), 256)
            right = rhi[:, cols]
            both = dot(ahi[...], right) + dot(alo[...], right) + dot(ahi[...], rlo[:, cols])
            mixed[2 * k] = both[:, :128]
            mixed[2 * k + 1] = both[:, 128:]
            return carry

        lax.fori_loop(0, NLON // 256, block, 0)

    def split_work():
        for t in range(TILES):
            high, low = split(work[t])
            ahi[:, t * 128 : (t + 1) * 128] = high
            alo[:, t * 128 : (t + 1) * 128] = low

    def send_forward(w, source):
        for level in range(LEVELS):
            for t in range(TILES):
                send[w, level * 4 + t // 2, :, (t % 2) * 128 : (t % 2 + 1) * 128] = source[
                    t, level_rows(level), :
                ]

        def go(k, carry):
            j = lax.rem(lat + k, LATS)
            pltpu.make_async_remote_copy(
                src_ref=send.at[w, j],
                dst_ref=recv.at[w, pl.ds(pl.multiple_of(lat * ROWS, ROWS), ROWS)],
                send_sem=fs_sem.at[w], recv_sem=fr_sem.at[w],
                device_id=(other, j), device_id_type=MESH,
            ).start()
            return carry

        lax.fori_loop(0, LATS, go, 0)

    def mix(w):
        pltpu.make_async_copy(recv.at[w], recv.at[w], fr_sem.at[w]).wait()

        def some(k, carry):
            rows = pl.ds(pl.multiple_of(k * 128, 128), 128)
            high, low = split(recv[w, rows, :])
            xhi[rows, :] = high
            xlo[rows, :] = low
            return carry

        lax.fori_loop(0, NLAT // 128, some, 0)

        def block(k, carry):
            first = lax.rem(lat // 8 + k, 4)
            rows = pl.ds(pl.multiple_of(first * 256, 256), 256)
            left = lhi[rows, :]
            back[w, rows, :] = (
                dot(left, xhi[...]) + dot(left, xlo[...]) + dot(llo[rows, :], xhi[...])
            )

            def go(i, inner):
                j = first * 8 + lax.rem(lat + i, 8)
                pltpu.make_async_remote_copy(
                    src_ref=back.at[w, pl.ds(pl.multiple_of(j * ROWS, ROWS), ROWS)],
                    dst_ref=ret.at[w, lat],
                    send_sem=bs_sem.at[w], recv_sem=br_sem.at[w],
                    device_id=(other, j), device_id_type=MESH,
                ).start()
                return inner

            lax.fori_loop(0, 8, go, 0)
            return carry

        lax.fori_loop(0, 4, block, 0)

    def finish_window(w, lon_done):
        pltpu.make_async_copy(ret.at[w], ret.at[w], br_sem.at[w]).wait()
        if lon_done:
            for level in range(LEVELS):
                for t in range(TILES):
                    work[t, level_rows(level), :] = ret[
                        w, level * 4 + t // 2, :, (t % 2) * 128 : (t % 2 + 1) * 128
                    ]
        else:
            for level in range(LEVELS):
                for quarter in range(4):
                    high, low = split(ret[w, level * 4 + quarter])
                    rows = slice(level * ROWS, (level + 1) * ROWS)
                    cols = slice(quarter * COLS, (quarter + 1) * COLS)
                    ahi[rows, cols] = high
                    alo[rows, cols] = low
            along_lon()
            for level in range(LEVELS):
                for t in range(TILES):
                    work[t, level_rows(level), :] = mixed[t, level * ROWS : (level + 1) * ROWS, :]

        def update(r, carry):
            rows = pl.ds(pl.multiple_of(r * LEVELS, LEVELS), LEVELS)
            applied = jnp.concatenate([work[t, rows, :] for t in range(TILES)], axis=1)
            field[w, r + STEPS] = field[w, r + STEPS] - 0.5 * applied
            return carry

        lax.fori_loop(0, ROWS, update, 0, unroll=2)
        pltpu.make_async_copy(
            field.at[w, pl.ds(STEPS, ROWS)], out.at[w], out_sem.at[w]
        ).start()

    loads[0].wait()
    loads[1].wait()
    interior(0, to_defect(1))
    for copy in halos:
        copy.wait_recv()
    for w in (3, 1, 2):
        window_halo(w)
    halo_of = {3: halos[6:8], 1: halos[8:10], 2: halos[10:12]}
    coefficients(1, STEPS)
    coefficients(STEPS + ROWS, EXT - 1)
    edges(0, to_defect(1))
    send_forward(1, work)

    loads[3].wait()
    integrate(3, to_ends)

    def send_ends(k, carry):
        rows = pl.ds(k * 2, 2)
        pltpu.make_async_remote_copy(
            src_ref=ends.at[rows], dst_ref=arrived.at[rows], send_sem=es_sem, recv_sem=er_sem,
            device_id=(nxt, lat), device_id_type=MESH,
        ).start()
        return carry

    lax.fori_loop(0, ROWS // 2, send_ends, 0)

    split_into(0, rhi, rlo)
    split_into(1, lhi, llo)

    loads[2].wait()
    integrate(1, to_defect(2))
    split_work()
    along_lon()
    send_forward(2, mixed)

    mix(1)

    integrate(2, to_defect(3))
    split_work()
    along_lon()
    send_forward(3, mixed)

    pltpu.make_async_copy(arrived, arrived, er_sem).wait()

    @pl.when(win == 0)
    def _():
        arrived[...] = jnp.zeros_like(arrived)

    def first_defect(r, carry):
        put_row(r, field[0, r + STEPS] - arrived[r])
        return carry

    lax.fori_loop(0, ROWS, first_defect, 0, unroll=2)
    split_work()
    along_lon()
    send_forward(0, mixed)

    mix(2)
    mix(3)
    mix(0)
    finish_window(1, False)
    finish_window(2, True)
    finish_window(3, True)
    finish_window(0, True)

    for copy in halos:
        copy.wait_send()

    pltpu.make_async_copy(ends, ends, es_sem).wait()

    for w in range(WINS):
        pltpu.make_async_copy(send.at[w], send.at[w], fs_sem.at[w]).wait()
        pltpu.make_async_copy(back.at[w], back.at[w], bs_sem.at[w]).wait()
        pltpu.make_async_copy(field.at[w, pl.ds(STEPS, ROWS)], out.at[w], out_sem.at[w]).wait()


def shards(increments, courant_lon, courant_lat, lat_factor, lon_factor):
    any_space = pl.BlockSpec(memory_space=pl.ANY)
    strip = (EXT, LEVELS, NLON)
    dma = pltpu.SemaphoreType.DMA
    return pl.pallas_call(
        kernel,
        out_shape=jax.ShapeDtypeStruct((WINS, ROWS, LEVELS, NLON), f32),
        in_specs=[any_space] * 5,
        out_specs=any_space,
        scratch_shapes=[
            pltpu.VMEM((WINS,) + strip, f32),
            pltpu.VMEM(strip, f32),
            pltpu.VMEM(strip, f32),
            pltpu.VMEM((EXT, LEVELS, 128), f32),
            pltpu.VMEM((EXT, LEVELS, 128), f32),
            pltpu.VMEM(strip, f32),
            pltpu.VMEM(strip, f32),
            pltpu.VMEM((2, NLAT, NLON), f32),
            pltpu.VMEM((NLAT, NLAT), bf16),
            pltpu.VMEM((NLAT, NLAT), bf16),
            pltpu.VMEM((NLON, NLON), bf16),
            pltpu.VMEM((NLON, NLON), bf16),
            pltpu.VMEM((ROWS, LEVELS, NLON), f32),
            pltpu.VMEM((ROWS, LEVELS, NLON), f32),
            pltpu.VMEM((TILES, ROWS * LEVELS, 128), f32),
            pltpu.VMEM((TILES, ROWS * LEVELS, 128), f32),
            pltpu.VMEM((ROWS * LEVELS, NLON), bf16),
            pltpu.VMEM((ROWS * LEVELS, NLON), bf16),
            pltpu.VMEM((NLAT, COLS), bf16),
            pltpu.VMEM((NLAT, COLS), bf16),
            pltpu.VMEM((WINS, LATS, ROWS, COLS), f32),
            pltpu.VMEM((WINS, NLAT, COLS), f32),
            pltpu.VMEM((WINS, NLAT, COLS), f32),
            pltpu.VMEM((WINS, LATS, ROWS, COLS), f32),
            dma((6,)),
            dma((2,)),
            dma((12,)),
            dma((12,)),
            dma,
            dma,
            dma((WINS,)),
            dma((WINS,)),
            dma((WINS,)),
            dma((WINS,)),
            dma((WINS,)),
        ],
        compiler_params=pltpu.CompilerParams(
            collective_id=0, has_side_effects=True, vmem_limit_bytes=60 << 20
        ),
        name="subwindows",
    )(increments, courant_lon, courant_lat, lat_factor, lon_factor)


def solution(mesh):
    in_specs = (P("win", "lat", None, None), P("lat", None, None), P("lat", None, None), P(), P())
    out_specs = P("win", "lat", None, None)
    return jax.shard_map(shards, mesh=mesh, in_specs=in_specs, out_specs=out_specs, check_vma=False)
```

```python
import math

import jax
import jax.numpy as jnp
from jax import lax
from jax.experimental import pallas as pl
from jax.experimental.pallas import tpu as pltpu
from jax.sharding import PartitionSpec as P

STEPS = 4
WINS = 4
ROWS = 32
LEVELS = 8
NLON = 1024
NLAT = 1024
LATS = 32
EXT = ROWS + 2 * STEPS
COLS = 256
TILES = NLON // 128
UNROLL = 2
MESH = pl.DeviceIdType.MESH

diffusion = 0.125
turning_scale = 0.6

f32 = jnp.float32
bf16 = jnp.bfloat16


def split(value):
    high = value.astype(bf16)
    low = (value - high.astype(f32)).astype(bf16)
    return high, low


def dot(a, b):
    return jnp.dot(a, b, preferred_element_type=f32)


def kernel(
    inc, clon, clat, lat_fac, lon_fac,
    out,
    field, co, cos_t, sin_t, odd_steps, even_steps,
    stage, lhi, llo, rhi, rlo,
    ends, arrived, work, mixed, ahi, alo, xhi, xlo,
    send, recv, back, ret,
    load_sem, stage_sem, hs_sem, hr_sem, es_sem, er_sem,
    fs_sem, fr_sem, bs_sem, br_sem, out_sem,
):
    lat = lax.axis_index("lat")
    win = lax.axis_index("win")
    other = lax.rem(win + 2, 4)
    north = lax.rem(lat + LATS - 1, LATS)
    south = lax.rem(lat + 1, LATS)
    nxt = lax.rem(win + 1, 4)
    prv = lax.rem(win + 3, 4)
    core = lax.rem(win, 2)
    sibling = win + 1 - 2 * core

    loads = []
    for w in range(WINS):
        loads.append(
            pltpu.make_async_copy(inc.at[w], field.at[w, pl.ds(STEPS, ROWS)], load_sem.at[w])
        )
    loads.append(pltpu.make_async_copy(clon, co.at[0, pl.ds(STEPS, ROWS)], load_sem.at[4]))
    loads.append(pltpu.make_async_copy(clat, co.at[1, pl.ds(STEPS, ROWS)], load_sem.at[5]))
    for copy in (loads[4], loads[5], loads[3], loads[0], loads[1], loads[2]):
        copy.start()
    factor_loads = [
        pltpu.make_async_copy(lon_fac, stage, stage_sem.at[0]),
        pltpu.make_async_copy(lat_fac, stage, stage_sem.at[1]),
    ]
    factor_loads[0].start()

    barrier = pltpu.get_barrier_semaphore()

    def greet(k, carry):
        pl.semaphore_signal(
            barrier, inc=1, device_id=(other, lax.rem(lat + k, LATS)), device_id_type=MESH
        )
        return carry

    for where in ((win, north), (win, south), (nxt, lat), (prv, lat)):
        pl.semaphore_signal(barrier, inc=1, device_id=where, device_id_type=MESH)
    lax.fori_loop(0, LATS, greet, 0)

    row = lax.broadcasted_iota(jnp.int32, (EXT, LEVELS, 128), 0) + (lat * ROWS - STEPS)
    inside = ((row >= 0) & (row < NLAT)).astype(f32)
    theta = turning_scale * jnp.cos(math.pi * (row.astype(f32) + 0.5) / NLAT)
    even3 = lax.rem(lax.broadcasted_iota(jnp.int32, (EXT, LEVELS, 128), 1), 2) == 0
    cos_t[...] = 0.5 * jnp.cos(theta) * inside
    sin_half = 0.5 * jnp.sin(theta) * inside
    sin_t[...] = jnp.where(even3, sin_half, -sin_half)

    def coefficients(r, carry):
        co[0, r] = 0.25 - co[0, r]
        co[1, r] = 0.25 - co[1, r]
        return carry

    loads[4].wait()
    loads[5].wait()
    lax.fori_loop(STEPS, STEPS + ROWS, coefficients, 0, unroll=2)

    pl.semaphore_wait(barrier, LATS + 4)

    halos = {}

    def courant_group(wraps):
        return jnp.where(wraps, other, win)

    def halo(src, dst, slot, where, group=None):
        copy = pltpu.make_async_remote_copy(
            src_ref=src, dst_ref=dst, send_sem=hs_sem.at[slot], recv_sem=hr_sem.at[slot],
            device_id=(win if group is None else group, where), device_id_type=MESH,
        )
        copy.start()
        halos[slot] = copy

    def window_halo(w):
        halo(inc.at[w, pl.ds(ROWS - STEPS, STEPS)], field.at[w, pl.ds(0, STEPS)], 2 * w, south)
        halo(inc.at[w, pl.ds(0, STEPS)], field.at[w, pl.ds(STEPS + ROWS, STEPS)], 2 * w + 1, north)

    def landed(*slots):
        for slot in slots:
            halos[slot].wait_recv()

    EDGE = STEPS - 1
    top = pl.ds(1, EDGE)
    bottom = pl.ds(STEPS + ROWS, EDGE)
    window_halo(3)
    halo(co.at[core, pl.ds(STEPS + ROWS - EDGE, EDGE)], co.at[core, top], 8, south,
         courant_group(lax.rem(lat, 4) == 3))
    halo(co.at[core, pl.ds(STEPS, EDGE)], co.at[core, bottom], 9, north,
         courant_group(lax.rem(lat, 4) == 0))
    window_halo(0)

    def hand_over():
        landed(8, 9)
        halo(co.at[core, top], co.at[core, top], 10, lat, sibling)
        halo(co.at[core, bottom], co.at[core, bottom], 11, lat, sibling)

    def split_into(slot, high_ref, low_ref):
        def some(k, carry):
            rows = pl.ds(pl.multiple_of(k * 32, 32), 32)
            high, low = split(stage[rows, :])
            high_ref[rows, :] = high
            low_ref[rows, :] = low
            return carry

        factor_loads[slot].wait()
        lax.fori_loop(0, NLAT // 32, some, 0)

    even = lax.rem(lax.broadcasted_iota(jnp.int32, (LEVELS, NLON), 0), 2) == 0

    def two_rows(src, r):
        near = [src[r - 1], src[r], src[r + 1], src[r + 2]]
        done = []
        for i in range(2):
            n, c, s = near[i : i + 3]
            e = pltpu.roll(c, NLON - 1, 1)
            w = pltpu.roll(c, 1, 1)
            y = (c + 0.5 * (w + n)) + co[0, r + i] * (e - w) + co[1, r + i] * (s - n)
            swapped = jnp.where(even, pltpu.roll(y, LEVELS - 1, 0), pltpu.roll(y, 1, 0))
            cosine = jnp.concatenate([cos_t[r + i]] * TILES, axis=1)
            sine = jnp.concatenate([sin_t[r + i]] * TILES, axis=1)
            done.append(cosine * y + sine * swapped)
        return done

    def advance(src, dst, first, last):
        def rows(k, carry):
            r = first + 2 * k
            dst[r], dst[r + 1] = two_rows(src, r)
            return carry

        lax.fori_loop(0, (last - first) // 2, rows, 0, unroll=UNROLL)

    def last_step(src, first, last, finish):
        def some(k, carry):
            r = first + 2 * k
            one, two = two_rows(src, r + STEPS)
            finish(r, one)
            finish(r + 1, two)
            return carry

        lax.fori_loop(0, (last - first) // 2, some, 0, unroll=UNROLL)

    def outside_is_zero(w):
        @pl.when(lat == 0)
        def _():
            field[w, 0:STEPS] = jnp.zeros((STEPS, LEVELS, NLON), f32)

        @pl.when(lat == LATS - 1)
        def _():
            field[w, STEPS + ROWS : EXT] = jnp.zeros((STEPS, LEVELS, NLON), f32)

    def stages(w, half):
        t1, t2 = odd_steps.at[half], even_steps.at[half]
        return (field.at[w], t1, 1), (t1, t2, 2), (t2, t1, 3)

    def integrate(w, finish):
        landed(2 * w, 2 * w + 1)
        outside_is_zero(w)
        for src, dst, step in stages(w, 0):
            advance(src, dst, step, EXT - step)
        last_step(odd_steps.at[0], 0, ROWS, finish)

    def interior(w, half, finish, between=None):
        for src, dst, step in stages(w, half):
            advance(src, dst, STEPS + step, EXT - STEPS - step)
            if step == 2 and between is not None:
                between()
        last_step(odd_steps.at[half], STEPS, ROWS - STEPS, finish)

    def edges(w, half, finish):
        outside_is_zero(w)
        for src, dst, step in stages(w, half):
            advance(src, dst, step, step + STEPS)
            advance(src, dst, EXT - step - STEPS, EXT - step)
        last_step(odd_steps.at[half], 0, STEPS, finish)
        last_step(odd_steps.at[half], ROWS - STEPS, ROWS, finish)

    def put_row(r, value):
        for t in range(TILES):
            work[t, pl.ds(pl.multiple_of(r * LEVELS, LEVELS), LEVELS), :] = value[
                :, t * 128 : (t + 1) * 128
            ]

    def level_rows(level):
        return pl.ds(level, ROWS, stride=LEVELS)

    def to_defect(w):
        def finish(r, value):
            put_row(r, field[w, r + STEPS] - value)

        return finish

    def to_ends(r, value):
        ends[r] = value

    def along_lon():
        def block(k, carry):
            cols = pl.ds(pl.multiple_of(k * 256, 256), 256)
            right = rhi[:, cols]
            both = dot(ahi[...], right) + dot(alo[...], right) + dot(ahi[...], rlo[:, cols])
            mixed[2 * k] = both[:, :128]
            mixed[2 * k + 1] = both[:, 128:]
            return carry

        lax.fori_loop(0, NLON // 256, block, 0)

    def split_work():
        for t in range(TILES):
            high, low = split(work[t])
            ahi[:, t * 128 : (t + 1) * 128] = high
            alo[:, t * 128 : (t + 1) * 128] = low

    def send_forward(w, source):
        for level in range(LEVELS):
            for t in range(TILES):
                send[w, level * 4 + t // 2, :, (t % 2) * 128 : (t % 2 + 1) * 128] = source[
                    t, level_rows(level), :
                ]

        def go(k, carry):
            j = lax.rem(lat + k, LATS)
            pltpu.make_async_remote_copy(
                src_ref=send.at[w, j],
                dst_ref=recv.at[w, pl.ds(pl.multiple_of(lat * ROWS, ROWS), ROWS)],
                send_sem=fs_sem.at[w], recv_sem=fr_sem.at[w],
                device_id=(other, j), device_id_type=MESH,
            ).start()
            return carry

        lax.fori_loop(0, LATS, go, 0)

    def mix(w):
        pltpu.make_async_copy(recv.at[w], recv.at[w], fr_sem.at[w]).wait()

        def some(k, carry):
            rows = pl.ds(pl.multiple_of(k * 128, 128), 128)
            high, low = split(recv[w, rows, :])
            xhi[rows, :] = high
            xlo[rows, :] = low
            return carry

        lax.fori_loop(0, NLAT // 128, some, 0)

        def block(k, carry):
            first = lax.rem(lat // 8 + k, 4)
            rows = pl.ds(pl.multiple_of(first * 256, 256), 256)
            left = lhi[rows, :]
            back[w, rows, :] = (
                dot(left, xhi[...]) + dot(left, xlo[...]) + dot(llo[rows, :], xhi[...])
            )

            def go(i, inner):
                j = first * 8 + lax.rem(lat + i, 8)
                pltpu.make_async_remote_copy(
                    src_ref=back.at[w, pl.ds(pl.multiple_of(j * ROWS, ROWS), ROWS)],
                    dst_ref=ret.at[w, lat],
                    send_sem=bs_sem.at[w], recv_sem=br_sem.at[w],
                    device_id=(other, j), device_id_type=MESH,
                ).start()
                return inner

            lax.fori_loop(0, 8, go, 0)
            return carry

        lax.fori_loop(0, 4, block, 0)

    def finish_window(w, lon_done):
        pltpu.make_async_copy(ret.at[w], ret.at[w], br_sem.at[w]).wait()
        if lon_done:
            for level in range(LEVELS):
                for t in range(TILES):
                    work[t, level_rows(level), :] = ret[
                        w, level * 4 + t // 2, :, (t % 2) * 128 : (t % 2 + 1) * 128
                    ]
        else:
            for level in range(LEVELS):
                for quarter in range(4):
                    high, low = split(ret[w, level * 4 + quarter])
                    rows = slice(level * ROWS, (level + 1) * ROWS)
                    cols = slice(quarter * COLS, (quarter + 1) * COLS)
                    ahi[rows, cols] = high
                    alo[rows, cols] = low
            along_lon()
            for level in range(LEVELS):
                for t in range(TILES):
                    work[t, level_rows(level), :] = mixed[t, level * ROWS : (level + 1) * ROWS, :]

        def update(r, carry):
            rows = pl.ds(pl.multiple_of(r * LEVELS, LEVELS), LEVELS)
            applied = jnp.concatenate([work[t, rows, :] for t in range(TILES)], axis=1)
            out[w, r] = field[w, r + STEPS] - 0.5 * applied
            return carry

        lax.fori_loop(0, ROWS, update, 0, unroll=2)

    def send_ends(first, last):
        def some(k, carry):
            rows = pl.ds(first + k * 2, 2)
            pltpu.make_async_remote_copy(
                src_ref=ends.at[rows], dst_ref=arrived.at[rows], send_sem=es_sem, recv_sem=er_sem,
                device_id=(nxt, lat), device_id_type=MESH,
            ).start()
            return carry

        lax.fori_loop(0, (last - first) // 2, some, 0)

    loads[3].wait()
    interior(3, 0, to_ends)
    loads[0].wait()
    loads[1].wait()
    interior(0, 1, to_defect(1), hand_over)
    landed(10, 11, 6, 7, 0, 1)
    window_halo(1)
    edges(3, 0, to_ends)
    send_ends(0, ROWS)
    edges(0, 1, to_defect(1))
    send_forward(1, work)
    window_halo(2)

    split_into(0, rhi, rlo)
    factor_loads[1].start()
    loads[2].wait()
    integrate(1, to_defect(2))
    split_work()
    along_lon()
    send_forward(2, mixed)

    pltpu.make_async_copy(arrived, arrived, er_sem).wait()

    @pl.when(win == 0)
    def _():
        arrived[...] = jnp.zeros_like(arrived)

    def first_defect(r, carry):
        put_row(r, field[0, r + STEPS] - arrived[r])
        return carry

    lax.fori_loop(0, ROWS, first_defect, 0, unroll=2)
    split_work()
    along_lon()
    send_forward(0, mixed)

    split_into(1, lhi, llo)
    mix(1)

    integrate(2, to_defect(3))
    split_work()
    along_lon()
    send_forward(3, mixed)

    mix(2)
    mix(0)
    mix(3)
    finish_window(1, False)
    finish_window(2, True)
    finish_window(0, True)
    finish_window(3, True)

    for copy in halos.values():
        copy.wait_send()

    pltpu.make_async_copy(ends, ends, es_sem).wait()

    for w in range(WINS):
        pltpu.make_async_copy(send.at[w], send.at[w], fs_sem.at[w]).wait()
        pltpu.make_async_copy(back.at[w], back.at[w], bs_sem.at[w]).wait()


def shards(increments, courant_lon, courant_lat, lat_factor, lon_factor):
    any_space = pl.BlockSpec(memory_space=pl.ANY)
    strip = (EXT, LEVELS, NLON)
    dma = pltpu.SemaphoreType.DMA
    return pl.pallas_call(
        kernel,
        out_shape=pltpu.VMEM((WINS, ROWS, LEVELS, NLON), f32),
        in_specs=[any_space] * 5,
        out_specs=pl.BlockSpec(memory_space=pltpu.VMEM),
        scratch_shapes=[
            pltpu.VMEM((WINS,) + strip, f32),
            pltpu.VMEM((2,) + strip, f32),
            pltpu.VMEM((EXT, LEVELS, 128), f32),
            pltpu.VMEM((EXT, LEVELS, 128), f32),
            pltpu.VMEM((2,) + strip, f32),
            pltpu.VMEM((2,) + strip, f32),
            pltpu.VMEM((NLAT, NLON), f32),
            pltpu.VMEM((NLAT, NLAT), bf16),
            pltpu.VMEM((NLAT, NLAT), bf16),
            pltpu.VMEM((NLON, NLON), bf16),
            pltpu.VMEM((NLON, NLON), bf16),
            pltpu.VMEM((ROWS, LEVELS, NLON), f32),
            pltpu.VMEM((ROWS, LEVELS, NLON), f32),
            pltpu.VMEM((TILES, ROWS * LEVELS, 128), f32),
            pltpu.VMEM((TILES, ROWS * LEVELS, 128), f32),
            pltpu.VMEM((ROWS * LEVELS, NLON), bf16),
            pltpu.VMEM((ROWS * LEVELS, NLON), bf16),
            pltpu.VMEM((NLAT, COLS), bf16),
            pltpu.VMEM((NLAT, COLS), bf16),
            pltpu.VMEM((WINS, LATS, ROWS, COLS), f32),
            pltpu.VMEM((WINS, NLAT, COLS), f32),
            pltpu.VMEM((WINS, NLAT, COLS), f32),
            pltpu.VMEM((WINS, LATS, ROWS, COLS), f32),
            dma((6,)),
            dma((2,)),
            dma((12,)),
            dma((12,)),
            dma,
            dma,
            dma((WINS,)),
            dma((WINS,)),
            dma((WINS,)),
            dma((WINS,)),
            dma((WINS,)),
        ],
        compiler_params=pltpu.CompilerParams(
            collective_id=0, has_side_effects=True, vmem_limit_bytes=54 << 20
        ),
        name="subwindows",
    )(increments, courant_lon, courant_lat, lat_factor, lon_factor)


def solution(mesh):
    in_specs = (P("win", "lat", None, None), P("lat", None, None), P("lat", None, None), P(), P())
    out_specs = P("win", "lat", None, None)
    return jax.shard_map(shards, mesh=mesh, in_specs=in_specs, out_specs=out_specs, check_vma=False)
```

```python
import math

import jax
import jax.numpy as jnp
from jax import lax
from jax.experimental import pallas as pl
from jax.experimental.pallas import tpu as pltpu
from jax.sharding import PartitionSpec as P

STEPS = 4
WINS = 4
ROWS = 32
LEVELS = 8
NLON = 1024
NLAT = 1024
LATS = 32
EXT = ROWS + 2 * STEPS
COLS = 256
TILES = NLON // 128
UNROLL = 2
MESH = pl.DeviceIdType.MESH

diffusion = 0.125
turning_scale = 0.6

f32 = jnp.float32
bf16 = jnp.bfloat16


def split(value):
    high = value.astype(bf16)
    low = (value - high.astype(f32)).astype(bf16)
    return high, low


def dot(a, b):
    return jnp.dot(a, b, preferred_element_type=f32)


def kernel(
    inc, clon, clat, lat_fac, lon_fac,
    out,
    field, co, cos_t, sin_t, odd_steps, even_steps,
    stage, lhi, llo, rhi, rlo,
    ends, arrived, work, mixed, ahi, alo, xhi, xlo,
    send, recv, back, ret, send_more, recv_more,
    load_sem, stage_sem, hs_sem, hr_sem, es_sem, er_sem,
    fs_sem, fr_sem, bs_sem, br_sem, ms_sem, mr_sem,
):
    lat = lax.axis_index("lat")
    win = lax.axis_index("win")
    other = lax.rem(win + 2, 4)
    north = lax.rem(lat + LATS - 1, LATS)
    south = lax.rem(lat + 1, LATS)
    core = lax.rem(win, 2)
    sibling = win + 1 - 2 * core

    loads = []
    for w in range(WINS):
        loads.append(
            pltpu.make_async_copy(inc.at[w], field.at[w, pl.ds(STEPS, ROWS)], load_sem.at[w])
        )
    loads.append(pltpu.make_async_copy(clon, co.at[0, pl.ds(STEPS, ROWS)], load_sem.at[4]))
    loads.append(pltpu.make_async_copy(clat, co.at[1, pl.ds(STEPS, ROWS)], load_sem.at[5]))
    for copy in (loads[4], loads[5], loads[0], loads[3], loads[1], loads[2]):
        copy.start()
    factor_loads = [
        pltpu.make_async_copy(lon_fac, stage, stage_sem.at[0]),
        pltpu.make_async_copy(lat_fac, stage, stage_sem.at[1]),
    ]
    factor_loads[0].start()

    barrier = pltpu.get_barrier_semaphore()

    def greet(k, carry):
        pl.semaphore_signal(
            barrier, inc=1, device_id=(other, lax.rem(lat + k, LATS)), device_id_type=MESH
        )
        return carry

    for where in ((win, north), (win, south), (sibling, lat)):
        pl.semaphore_signal(barrier, inc=1, device_id=where, device_id_type=MESH)
    lax.fori_loop(0, LATS, greet, 0)

    def greet_more(k, carry):
        pl.semaphore_signal(
            barrier, inc=1, device_id=(1, lax.rem(lat + k, LATS)), device_id_type=MESH
        )
        return carry

    @pl.when(win == 0)
    def _():
        lax.fori_loop(0, LATS, greet_more, 0)

    row = lax.broadcasted_iota(jnp.int32, (EXT, LEVELS, 128), 0) + (lat * ROWS - STEPS)
    inside = ((row >= 0) & (row < NLAT)).astype(f32)
    theta = turning_scale * jnp.cos(math.pi * (row.astype(f32) + 0.5) / NLAT)
    even3 = lax.rem(lax.broadcasted_iota(jnp.int32, (EXT, LEVELS, 128), 1), 2) == 0
    cos_t[...] = 0.5 * jnp.cos(theta) * inside
    sin_half = 0.5 * jnp.sin(theta) * inside
    sin_t[...] = jnp.where(even3, sin_half, -sin_half)

    def coefficients(r, carry):
        co[0, r] = 0.25 - co[0, r]
        co[1, r] = 0.25 - co[1, r]
        return carry

    loads[4].wait()
    loads[5].wait()
    lax.fori_loop(STEPS, STEPS + ROWS, coefficients, 0, unroll=2)

    @pl.when(win == 1)
    def _():
        pl.semaphore_wait(barrier, 2 * LATS + 3)

    @pl.when(win != 1)
    def _():
        pl.semaphore_wait(barrier, LATS + 3)

    halos = {}

    def courant_group(wraps):
        return jnp.where(wraps, other, win)

    def halo(src, dst, slot, where, group=None):
        copy = pltpu.make_async_remote_copy(
            src_ref=src, dst_ref=dst, send_sem=hs_sem.at[slot], recv_sem=hr_sem.at[slot],
            device_id=(win if group is None else group, where), device_id_type=MESH,
        )
        copy.start()
        halos[slot] = copy

    def window_halo(w):
        halo(inc.at[w, pl.ds(ROWS - STEPS, STEPS)], field.at[w, pl.ds(0, STEPS)], 2 * w, south)
        halo(inc.at[w, pl.ds(0, STEPS)], field.at[w, pl.ds(STEPS + ROWS, STEPS)], 2 * w + 1, north)

    def landed(*slots):
        for slot in slots:
            halos[slot].wait_recv()

    EDGE = STEPS - 1
    top = pl.ds(1, EDGE)
    bottom = pl.ds(STEPS + ROWS, EDGE)
    window_halo(3)
    halo(co.at[core, pl.ds(STEPS + ROWS - EDGE, EDGE)], co.at[core, top], 8, south,
         courant_group(lax.rem(lat, 4) == 3))
    halo(co.at[core, pl.ds(STEPS, EDGE)], co.at[core, bottom], 9, north,
         courant_group(lax.rem(lat, 4) == 0))
    window_halo(0)

    def hand_over():
        landed(8, 9)
        halo(co.at[core, top], co.at[core, top], 10, lat, sibling)
        halo(co.at[core, bottom], co.at[core, bottom], 11, lat, sibling)

    def split_into(slot, high_ref, low_ref):
        def some(k, carry):
            rows = pl.ds(pl.multiple_of(k * 32, 32), 32)
            high, low = split(stage[rows, :])
            high_ref[rows, :] = high
            low_ref[rows, :] = low
            return carry

        factor_loads[slot].wait()
        lax.fori_loop(0, NLAT // 32, some, 0)

    even = lax.rem(lax.broadcasted_iota(jnp.int32, (LEVELS, NLON), 0), 2) == 0

    def two_rows(src, r):
        near = [src[r - 1], src[r], src[r + 1], src[r + 2]]
        done = []
        for i in range(2):
            n, c, s = near[i : i + 3]
            e = pltpu.roll(c, NLON - 1, 1)
            w = pltpu.roll(c, 1, 1)
            y = (c + 0.5 * (w + n)) + co[0, r + i] * (e - w) + co[1, r + i] * (s - n)
            swapped = jnp.where(even, pltpu.roll(y, LEVELS - 1, 0), pltpu.roll(y, 1, 0))
            cosine = jnp.concatenate([cos_t[r + i]] * TILES, axis=1)
            sine = jnp.concatenate([sin_t[r + i]] * TILES, axis=1)
            done.append(cosine * y + sine * swapped)
        return done

    def advance(src, dst, first, last):
        def rows(k, carry):
            r = first + 2 * k
            dst[r], dst[r + 1] = two_rows(src, r)
            return carry

        lax.fori_loop(0, (last - first) // 2, rows, 0, unroll=UNROLL)

    def last_step(src, first, last, finish):
        def some(k, carry):
            r = first + 2 * k
            one, two = two_rows(src, r + STEPS)
            finish(r, one)
            finish(r + 1, two)
            return carry

        lax.fori_loop(0, (last - first) // 2, some, 0, unroll=UNROLL)

    def outside_is_zero(w):
        @pl.when(lat == 0)
        def _():
            field[w, 0:STEPS] = jnp.zeros((STEPS, LEVELS, NLON), f32)

        @pl.when(lat == LATS - 1)
        def _():
            field[w, STEPS + ROWS : EXT] = jnp.zeros((STEPS, LEVELS, NLON), f32)

    def stages(w, half):
        t1, t2 = odd_steps.at[half], even_steps.at[half]
        return (field.at[w], t1, 1), (t1, t2, 2), (t2, t1, 3)

    def integrate(w, finish):
        landed(2 * w, 2 * w + 1)
        outside_is_zero(w)
        for src, dst, step in stages(w, 0):
            advance(src, dst, step, EXT - step)
        last_step(odd_steps.at[0], 0, ROWS, finish)

    def interior(w, half, finish, between=None):
        for src, dst, step in stages(w, half):
            advance(src, dst, STEPS + step, EXT - STEPS - step)
            if step == 2 and between is not None:
                between()
        last_step(odd_steps.at[half], STEPS, ROWS - STEPS, finish)

    def edges(w, half, finish):
        outside_is_zero(w)
        for src, dst, step in stages(w, half):
            advance(src, dst, step, step + STEPS)
            advance(src, dst, EXT - step - STEPS, EXT - step)
        last_step(odd_steps.at[half], 0, STEPS, finish)
        last_step(odd_steps.at[half], ROWS - STEPS, ROWS, finish)

    def put_row(r, value, target=None):
        target = work if target is None else target
        for t in range(TILES):
            target[t, pl.ds(pl.multiple_of(r * LEVELS, LEVELS), LEVELS), :] = value[
                :, t * 128 : (t + 1) * 128
            ]

    def level_rows(level):
        return pl.ds(level, ROWS, stride=LEVELS)

    def to_defect(w):
        def finish(r, value):
            put_row(r, field[w, r + STEPS] - value)

        return finish

    def to_ends(r, value):
        put_row(r, value, ends)

    def along_lon():
        def block(k, carry):
            cols = pl.ds(pl.multiple_of(k * 256, 256), 256)
            right = rhi[:, cols]
            both = dot(ahi[...], right) + dot(alo[...], right) + dot(ahi[...], rlo[:, cols])
            mixed[2 * k] = both[:, :128]
            mixed[2 * k + 1] = both[:, 128:]
            return carry

        lax.fori_loop(0, NLON // 256, block, 0)

    def split_work():
        for t in range(TILES):
            high, low = split(work[t])
            ahi[:, t * 128 : (t + 1) * 128] = high
            alo[:, t * 128 : (t + 1) * 128] = low

    def by_level(source, target):
        for level in range(LEVELS):
            for t in range(TILES):
                target[level * 4 + t // 2, :, (t % 2) * 128 : (t % 2 + 1) * 128] = source[
                    t, level_rows(level), :
                ]

    def send_end_state():
        by_level(ends, send_more)

        def go(k, carry):
            j = lax.rem(lat + k, LATS)
            pltpu.make_async_remote_copy(
                src_ref=send_more.at[j],
                dst_ref=recv_more.at[pl.ds(pl.multiple_of(lat * ROWS, ROWS), ROWS)],
                send_sem=ms_sem, recv_sem=mr_sem,
                device_id=(0, j), device_id_type=MESH,
            ).start()
            return carry

        lax.fori_loop(0, LATS, go, 0)

    def send_forward(w, source):
        by_level(source, send.at[w])

        def go(k, carry):
            j = lax.rem(lat + k, LATS)
            pltpu.make_async_remote_copy(
                src_ref=send.at[w, j],
                dst_ref=recv.at[w, pl.ds(pl.multiple_of(lat * ROWS, ROWS), ROWS)],
                send_sem=fs_sem.at[w], recv_sem=fr_sem.at[w],
                device_id=(other, j), device_id_type=MESH,
            ).start()
            return carry

        lax.fori_loop(0, LATS, go, 0)

    def mix(w, hold=False, here=False):
        if not here:
            pltpu.make_async_copy(recv.at[w], recv.at[w], fr_sem.at[w]).wait()

        def some(k, carry):
            rows = pl.ds(pl.multiple_of(k * 128, 128), 128)
            high, low = split(recv[w, rows, :])
            xhi[rows, :] = high
            xlo[rows, :] = low
            return carry

        lax.fori_loop(0, NLAT // 128, some, 0)

        def block(k, carry):
            first = lax.rem(lat // 8 + k, 4)
            rows = pl.ds(pl.multiple_of(first * 256, 256), 256)
            left = lhi[rows, :]
            back[w, rows, :] = (
                dot(left, xhi[...]) + dot(left, xlo[...]) + dot(llo[rows, :], xhi[...])
            )

            def go(i, inner):
                j = first * 8 + lax.rem(lat + i, 8)
                pltpu.make_async_remote_copy(
                    src_ref=back.at[w, pl.ds(pl.multiple_of(j * ROWS, ROWS), ROWS)],
                    dst_ref=ret.at[w, lat],
                    send_sem=bs_sem.at[w], recv_sem=br_sem.at[w],
                    device_id=(other, j), device_id_type=MESH,
                ).start()
                return inner

            if not hold:
                lax.fori_loop(0, 8, go, 0)
            return carry

        lax.fori_loop(0, 4, block, 0)

    def send_back(w):
        def go(k, carry):
            j = lax.rem(lat + k, LATS)
            pltpu.make_async_remote_copy(
                src_ref=back.at[w, pl.ds(pl.multiple_of(j * ROWS, ROWS), ROWS)],
                dst_ref=ret.at[w, lat],
                send_sem=bs_sem.at[w], recv_sem=br_sem.at[w],
                device_id=(other, j), device_id_type=MESH,
            ).start()
            return carry

        lax.fori_loop(0, LATS, go, 0)

    def rows_sent(w):
        pltpu.make_async_copy(back.at[w], back.at[w], bs_sem.at[w]).wait()

    def forward_sent(w):
        pltpu.make_async_copy(send.at[w], send.at[w], fs_sem.at[w]).wait()

    def finish_window(w, lon_done):
        pltpu.make_async_copy(ret.at[w], ret.at[w], br_sem.at[w]).wait()
        if lon_done:
            for level in range(LEVELS):
                for t in range(TILES):
                    work[t, level_rows(level), :] = ret[
                        w, level * 4 + t // 2, :, (t % 2) * 128 : (t % 2 + 1) * 128
                    ]
        else:
            for level in range(LEVELS):
                for quarter in range(4):
                    high, low = split(ret[w, level * 4 + quarter])
                    rows = slice(level * ROWS, (level + 1) * ROWS)
                    cols = slice(quarter * COLS, (quarter + 1) * COLS)
                    ahi[rows, cols] = high
                    alo[rows, cols] = low
            along_lon()
            for level in range(LEVELS):
                for t in range(TILES):
                    work[t, level_rows(level), :] = mixed[t, level * ROWS : (level + 1) * ROWS, :]

        def update(r, carry):
            rows = pl.ds(pl.multiple_of(r * LEVELS, LEVELS), LEVELS)
            applied = jnp.concatenate([work[t, rows, :] for t in range(TILES)], axis=1)
            out[w, r] = field[w, r + STEPS] - 0.5 * applied
            return carry

        lax.fori_loop(0, ROWS, update, 0, unroll=2)

    ends_copy = pltpu.make_async_remote_copy(
        src_ref=ends, dst_ref=arrived, send_sem=es_sem, recv_sem=er_sem,
        device_id=(sibling, lat), device_id_type=MESH,
    )

    loads[0].wait()

    @pl.when(core == 0)
    def _():
        def copy_row(r, carry):
            put_row(r, field[0, r + STEPS])
            return carry

        lax.fori_loop(0, ROWS, copy_row, 0, unroll=2)
        send_forward(0, work)

    loads[3].wait()
    interior(3, 0, to_ends)
    loads[1].wait()
    interior(0, 1, to_defect(1), hand_over)
    landed(10, 11, 6, 7, 0, 1)
    window_halo(1)
    edges(3, 0, to_ends)

    @pl.when(core == 0)
    def _():
        ends_copy.start()

    edges(0, 1, to_defect(1))
    send_forward(1, work)
    window_halo(2)

    @pl.when(core == 1)
    def _():
        ends_copy.wait_recv()

        def first_defect(r, carry):
            rows = pl.ds(pl.multiple_of(r * LEVELS, LEVELS), LEVELS)
            before = jnp.concatenate([arrived[t, rows, :] for t in range(TILES)], axis=1)
            put_row(r, field[0, r + STEPS] - before)
            return carry

        lax.fori_loop(0, ROWS, first_defect, 0, unroll=2)
        send_forward(0, work)

    @pl.when(win == 1)
    def _():
        send_end_state()

    split_into(0, rhi, rlo)
    factor_loads[1].start()
    loads[2].wait()
    integrate(1, to_defect(2))
    split_work()
    along_lon()
    send_forward(2, mixed)

    integrate(2, to_defect(3))
    split_work()
    along_lon()
    send_forward(3, mixed)
    split_into(1, lhi, llo)
    mix(1, hold=True)

    mix(2, hold=True)

    @pl.when(win == 0)
    def _():
        pltpu.make_async_copy(recv_more, recv_more, mr_sem).wait()
        pltpu.make_async_copy(recv.at[0], recv.at[0], fr_sem.at[0]).wait()

        def subtract(k, carry):
            rows = pl.ds(pl.multiple_of(k * 64, 64), 64)
            recv[0, rows, :] = recv[0, rows, :] - recv_more[rows, :]
            return carry

        lax.fori_loop(0, NLAT // 64, subtract, 0)

    @pl.when(win != 0)
    def _():
        pltpu.make_async_copy(recv.at[0], recv.at[0], fr_sem.at[0]).wait()

    mix(0, hold=True, here=True)
    for w in (1, 2, 0, 3):
        forward_sent(w)

    send_back(1)
    send_back(2)
    mix(3, hold=True)
    rows_sent(1)
    send_back(0)
    finish_window(1, False)
    rows_sent(2)
    send_back(3)
    finish_window(2, True)
    finish_window(0, False)
    finish_window(3, True)
    rows_sent(0)
    rows_sent(3)

    for copy in halos.values():
        copy.wait_send()

    @pl.when(core == 0)
    def _():
        ends_copy.wait_send()

    @pl.when(win == 1)
    def _():
        pltpu.make_async_copy(send_more, send_more, ms_sem).wait()


def shards(increments, courant_lon, courant_lat, lat_factor, lon_factor):
    any_space = pl.BlockSpec(memory_space=pl.ANY)
    strip = (EXT, LEVELS, NLON)
    dma = pltpu.SemaphoreType.DMA
    return pl.pallas_call(
        kernel,
        out_shape=pltpu.VMEM((WINS, ROWS, LEVELS, NLON), f32),
        in_specs=[any_space] * 5,
        out_specs=pl.BlockSpec(memory_space=pltpu.VMEM),
        scratch_shapes=[
            pltpu.VMEM((WINS,) + strip, f32),
            pltpu.VMEM((2,) + strip, f32),
            pltpu.VMEM((EXT, LEVELS, 128), f32),
            pltpu.VMEM((EXT, LEVELS, 128), f32),
            pltpu.VMEM((2,) + strip, f32),
            pltpu.VMEM((2,) + strip, f32),
            pltpu.VMEM((NLAT, NLON), f32),
            pltpu.VMEM((NLAT, NLAT), bf16),
            pltpu.VMEM((NLAT, NLAT), bf16),
            pltpu.VMEM((NLON, NLON), bf16),
            pltpu.VMEM((NLON, NLON), bf16),
            pltpu.VMEM((TILES, ROWS * LEVELS, 128), f32),
            pltpu.VMEM((TILES, ROWS * LEVELS, 128), f32),
            pltpu.VMEM((TILES, ROWS * LEVELS, 128), f32),
            pltpu.VMEM((TILES, ROWS * LEVELS, 128), f32),
            pltpu.VMEM((ROWS * LEVELS, NLON), bf16),
            pltpu.VMEM((ROWS * LEVELS, NLON), bf16),
            pltpu.VMEM((NLAT, COLS), bf16),
            pltpu.VMEM((NLAT, COLS), bf16),
            pltpu.VMEM((WINS, LATS, ROWS, COLS), f32),
            pltpu.VMEM((WINS, NLAT, COLS), f32),
            pltpu.VMEM((WINS, NLAT, COLS), f32),
            pltpu.VMEM((WINS, LATS, ROWS, COLS), f32),
            pltpu.VMEM((LATS, ROWS, COLS), f32),
            pltpu.VMEM((NLAT, COLS), f32),
            dma((6,)),
            dma((2,)),
            dma((12,)),
            dma((12,)),
            dma,
            dma,
            dma((WINS,)),
            dma((WINS,)),
            dma((WINS,)),
            dma((WINS,)),
            dma,
            dma,
        ],
        compiler_params=pltpu.CompilerParams(
            collective_id=0, has_side_effects=True, vmem_limit_bytes=56 << 20
        ),
        name="subwindows",
    )(increments, courant_lon, courant_lat, lat_factor, lon_factor)


def solution(mesh):
    in_specs = (P("win", "lat", None, None), P("lat", None, None), P("lat", None, None), P(), P())
    out_specs = P("win", "lat", None, None)
    return jax.shard_map(shards, mesh=mesh, in_specs=in_specs, out_specs=out_specs, check_vma=False)
```

```python
import math

import jax
import jax.numpy as jnp
from jax import lax
from jax.experimental import pallas as pl
from jax.experimental.pallas import tpu as pltpu
from jax.sharding import PartitionSpec as P

STEPS = 4
WINS = 4
ROWS = 32
LEVELS = 8
NLON = 1024
NLAT = 1024
LATS = 32
EXT = ROWS + 2 * STEPS
COLS = 256
TILES = NLON // 128
UNROLL = 2
MESH = pl.DeviceIdType.MESH

diffusion = 0.125
turning_scale = 0.6

f32 = jnp.float32
bf16 = jnp.bfloat16


def split(value):
    high = value.astype(bf16)
    low = (value - high.astype(f32)).astype(bf16)
    return high, low


def dot(a, b):
    return jnp.dot(a, b, preferred_element_type=f32)


def kernel(
    inc, clon, clat, lat_fac, lon_fac,
    out,
    field, co, cos_t, sin_t, odd_steps, even_steps,
    stage, lhi, llo, rhi, rlo,
    ends, arrived, work, mixed, ahi, alo, xhi, xlo,
    send, recv, back, ret, send_more, recv_more,
    load_sem, stage_sem, hs_sem, hr_sem, es_sem, er_sem,
    fs_sem, fr_sem, bs_sem, br_sem, ms_sem, mr_sem,
):
    lat = lax.axis_index("lat")
    win = lax.axis_index("win")
    other = lax.rem(win + 2, 4)
    north = lax.rem(lat + LATS - 1, LATS)
    south = lax.rem(lat + 1, LATS)
    core = lax.rem(win, 2)
    sibling = win + 1 - 2 * core

    loads = []
    for w in range(WINS):
        loads.append(
            pltpu.make_async_copy(inc.at[w], field.at[w, pl.ds(STEPS, ROWS)], load_sem.at[w])
        )
    loads.append(pltpu.make_async_copy(clon, co.at[0, pl.ds(STEPS, ROWS)], load_sem.at[4]))
    loads.append(pltpu.make_async_copy(clat, co.at[1, pl.ds(STEPS, ROWS)], load_sem.at[5]))
    for copy in (loads[4], loads[5], loads[0], loads[3], loads[1], loads[2]):
        copy.start()
    factor_loads = [
        pltpu.make_async_copy(lon_fac, stage, stage_sem.at[0]),
        pltpu.make_async_copy(lat_fac, stage, stage_sem.at[1]),
    ]
    factor_loads[0].start()

    barrier = pltpu.get_barrier_semaphore()

    def greet(k, carry):
        pl.semaphore_signal(
            barrier, inc=1, device_id=(other, lax.rem(lat + k, LATS)), device_id_type=MESH
        )
        return carry

    for where in ((win, north), (win, south), (sibling, lat)):
        pl.semaphore_signal(barrier, inc=1, device_id=where, device_id_type=MESH)
    lax.fori_loop(0, LATS, greet, 0)

    def greet_more(k, carry):
        pl.semaphore_signal(
            barrier, inc=1, device_id=(1, lax.rem(lat + k, LATS)), device_id_type=MESH
        )
        return carry

    @pl.when(win == 0)
    def _():
        lax.fori_loop(0, LATS, greet_more, 0)

    row = lax.broadcasted_iota(jnp.int32, (EXT, LEVELS, 128), 0) + (lat * ROWS - STEPS)
    inside = ((row >= 0) & (row < NLAT)).astype(f32)
    theta = turning_scale * jnp.cos(math.pi * (row.astype(f32) + 0.5) / NLAT)
    even3 = lax.rem(lax.broadcasted_iota(jnp.int32, (EXT, LEVELS, 128), 1), 2) == 0
    cos_t[...] = 0.5 * jnp.cos(theta) * inside
    sin_half = 0.5 * jnp.sin(theta) * inside
    sin_t[...] = jnp.where(even3, sin_half, -sin_half)

    def coefficients(r, carry):
        co[0, r] = 0.25 - co[0, r]
        co[1, r] = 0.25 - co[1, r]
        return carry

    loads[4].wait()
    loads[5].wait()
    lax.fori_loop(STEPS, STEPS + ROWS, coefficients, 0, unroll=2)

    @pl.when(win == 1)
    def _():
        pl.semaphore_wait(barrier, 2 * LATS + 3)

    @pl.when(win != 1)
    def _():
        pl.semaphore_wait(barrier, LATS + 3)

    halos = {}

    def courant_group(wraps):
        return jnp.where(wraps, other, win)

    def halo(src, dst, slot, where, group=None):
        copy = pltpu.make_async_remote_copy(
            src_ref=src, dst_ref=dst, send_sem=hs_sem.at[slot], recv_sem=hr_sem.at[slot],
            device_id=(win if group is None else group, where), device_id_type=MESH,
        )
        copy.start()
        halos[slot] = copy

    def window_halo(w):
        halo(inc.at[w, pl.ds(ROWS - STEPS, STEPS)], field.at[w, pl.ds(0, STEPS)], 2 * w, south)
        halo(inc.at[w, pl.ds(0, STEPS)], field.at[w, pl.ds(STEPS + ROWS, STEPS)], 2 * w + 1, north)

    def landed(*slots):
        for slot in slots:
            halos[slot].wait_recv()

    EDGE = STEPS - 1
    top = pl.ds(1, EDGE)
    bottom = pl.ds(STEPS + ROWS, EDGE)
    window_halo(3)
    halo(co.at[core, pl.ds(STEPS + ROWS - EDGE, EDGE)], co.at[core, top], 8, south,
         courant_group(lax.rem(lat, 4) == 3))
    halo(co.at[core, pl.ds(STEPS, EDGE)], co.at[core, bottom], 9, north,
         courant_group(lax.rem(lat, 4) == 0))
    window_halo(0)

    def hand_over():
        landed(8, 9)
        halo(co.at[core, top], co.at[core, top], 10, lat, sibling)
        halo(co.at[core, bottom], co.at[core, bottom], 11, lat, sibling)

    def split_into(slot, high_ref, low_ref):
        def some(k, carry):
            rows = pl.ds(pl.multiple_of(k * 32, 32), 32)
            high, low = split(stage[rows, :])
            high_ref[rows, :] = high
            low_ref[rows, :] = low
            return carry

        factor_loads[slot].wait()
        lax.fori_loop(0, NLAT // 32, some, 0)

    even = lax.rem(lax.broadcasted_iota(jnp.int32, (LEVELS, NLON), 0), 2) == 0

    def two_rows(src, r):
        near = [src[r - 1], src[r], src[r + 1], src[r + 2]]
        done = []
        for i in range(2):
            n, c, s = near[i : i + 3]
            e = pltpu.roll(c, NLON - 1, 1)
            w = pltpu.roll(c, 1, 1)
            y = (c + 0.5 * (w + n)) + co[0, r + i] * (e - w) + co[1, r + i] * (s - n)
            swapped = jnp.where(even, pltpu.roll(y, LEVELS - 1, 0), pltpu.roll(y, 1, 0))
            cosine = jnp.concatenate([cos_t[r + i]] * TILES, axis=1)
            sine = jnp.concatenate([sin_t[r + i]] * TILES, axis=1)
            done.append(cosine * y + sine * swapped)
        return done

    def advance(src, dst, first, last):
        def rows(k, carry):
            r = first + 2 * k
            dst[r], dst[r + 1] = two_rows(src, r)
            return carry

        lax.fori_loop(0, (last - first) // 2, rows, 0, unroll=UNROLL)

    def last_step(src, first, last, finish):
        def some(k, carry):
            r = first + 2 * k
            one, two = two_rows(src, r + STEPS)
            finish(r, one)
            finish(r + 1, two)
            return carry

        lax.fori_loop(0, (last - first) // 2, some, 0, unroll=UNROLL)

    def outside_is_zero(w):
        @pl.when(lat == 0)
        def _():
            field[w, 0:STEPS] = jnp.zeros((STEPS, LEVELS, NLON), f32)

        @pl.when(lat == LATS - 1)
        def _():
            field[w, STEPS + ROWS : EXT] = jnp.zeros((STEPS, LEVELS, NLON), f32)

    def stages(w, half):
        t1, t2 = odd_steps.at[half], even_steps.at[half]
        return (field.at[w], t1, 1), (t1, t2, 2), (t2, t1, 3)

    def integrate(w, finish):
        landed(2 * w, 2 * w + 1)
        outside_is_zero(w)
        for src, dst, step in stages(w, 0):
            advance(src, dst, step, EXT - step)
        last_step(odd_steps.at[0], 0, ROWS, finish)

    def interior(w, half, finish, between=None):
        for src, dst, step in stages(w, half):
            advance(src, dst, STEPS + step, EXT - STEPS - step)
            if step == 2 and between is not None:
                between()
        last_step(odd_steps.at[half], STEPS, ROWS - STEPS, finish)

    def edges(w, half, finish):
        outside_is_zero(w)
        for src, dst, step in stages(w, half):
            advance(src, dst, step, step + STEPS)
            advance(src, dst, EXT - step - STEPS, EXT - step)
        last_step(odd_steps.at[half], 0, STEPS, finish)
        last_step(odd_steps.at[half], ROWS - STEPS, ROWS, finish)

    def put_row(r, value, target=None):
        target = work if target is None else target
        for t in range(TILES):
            target[t, pl.ds(pl.multiple_of(r * LEVELS, LEVELS), LEVELS), :] = value[
                :, t * 128 : (t + 1) * 128
            ]

    def level_rows(level):
        return pl.ds(level, ROWS, stride=LEVELS)

    def to_defect(w):
        def finish(r, value):
            put_row(r, field[w, r + STEPS] - value)

        return finish

    def to_ends(r, value):
        put_row(r, value, ends)

    def along_lon():
        def block(k, carry):
            cols = pl.ds(pl.multiple_of(k * 256, 256), 256)
            right = rhi[:, cols]
            both = dot(ahi[...], right) + dot(alo[...], right) + dot(ahi[...], rlo[:, cols])
            mixed[2 * k] = both[:, :128]
            mixed[2 * k + 1] = both[:, 128:]
            return carry

        lax.fori_loop(0, NLON // 256, block, 0)

    def split_work():
        for t in range(TILES):
            high, low = split(work[t])
            ahi[:, t * 128 : (t + 1) * 128] = high
            alo[:, t * 128 : (t + 1) * 128] = low

    def by_level(source, target):
        for level in range(LEVELS):
            for t in range(TILES):
                target[level * 4 + t // 2, :, (t % 2) * 128 : (t % 2 + 1) * 128] = source[
                    t, level_rows(level), :
                ]

    def send_end_state():
        by_level(ends, send_more)

        def go(k, carry):
            j = lax.rem(lat + k, LATS)
            pltpu.make_async_remote_copy(
                src_ref=send_more.at[j],
                dst_ref=recv_more.at[pl.ds(pl.multiple_of(lat * ROWS, ROWS), ROWS)],
                send_sem=ms_sem, recv_sem=mr_sem,
                device_id=(0, j), device_id_type=MESH,
            ).start()
            return carry

        lax.fori_loop(0, LATS, go, 0)

    def send_forward(w, source):
        by_level(source, send.at[w])

        def go(k, carry):
            j = lax.rem(lat + k, LATS)
            pltpu.make_async_remote_copy(
                src_ref=send.at[w, j],
                dst_ref=recv.at[w, pl.ds(pl.multiple_of(lat * ROWS, ROWS), ROWS)],
                send_sem=fs_sem.at[w], recv_sem=fr_sem.at[w],
                device_id=(other, j), device_id_type=MESH,
            ).start()
            return carry

        lax.fori_loop(0, LATS, go, 0)

    def mix(w, hold=False, here=False):
        if not here:
            pltpu.make_async_copy(recv.at[w], recv.at[w], fr_sem.at[w]).wait()

        def some(k, carry):
            rows = pl.ds(pl.multiple_of(k * 128, 128), 128)
            high, low = split(recv[w, rows, :])
            xhi[rows, :] = high
            xlo[rows, :] = low
            return carry

        lax.fori_loop(0, NLAT // 128, some, 0)

        def block(k, carry):
            first = lax.rem(lat // 8 + k, 4)
            rows = pl.ds(pl.multiple_of(first * 256, 256), 256)
            left = lhi[rows, :]
            back[w, rows, :] = (
                dot(left, xhi[...]) + dot(left, xlo[...]) + dot(llo[rows, :], xhi[...])
            )

            def go(i, inner):
                j = first * 8 + lax.rem(lat + i, 8)
                pltpu.make_async_remote_copy(
                    src_ref=back.at[w, pl.ds(pl.multiple_of(j * ROWS, ROWS), ROWS)],
                    dst_ref=ret.at[w, lat],
                    send_sem=bs_sem.at[w], recv_sem=br_sem.at[w],
                    device_id=(other, j), device_id_type=MESH,
                ).start()
                return inner

            if not hold:
                lax.fori_loop(0, 8, go, 0)
            return carry

        lax.fori_loop(0, 4, block, 0)

    def send_back(w):
        def go(k, carry):
            j = lax.rem(lat + k, LATS)
            pltpu.make_async_remote_copy(
                src_ref=back.at[w, pl.ds(pl.multiple_of(j * ROWS, ROWS), ROWS)],
                dst_ref=ret.at[w, lat],
                send_sem=bs_sem.at[w], recv_sem=br_sem.at[w],
                device_id=(other, j), device_id_type=MESH,
            ).start()
            return carry

        lax.fori_loop(0, LATS, go, 0)

    def rows_sent(w):
        pltpu.make_async_copy(back.at[w], back.at[w], bs_sem.at[w]).wait()

    def forward_sent(w):
        pltpu.make_async_copy(send.at[w], send.at[w], fs_sem.at[w]).wait()

    def finish_window(w, lon_done):
        pltpu.make_async_copy(ret.at[w], ret.at[w], br_sem.at[w]).wait()
        if lon_done:
            for level in range(LEVELS):
                for t in range(TILES):
                    work[t, level_rows(level), :] = ret[
                        w, level * 4 + t // 2, :, (t % 2) * 128 : (t % 2 + 1) * 128
                    ]
        else:
            for level in range(LEVELS):
                for quarter in range(4):
                    high, low = split(ret[w, level * 4 + quarter])
                    rows = slice(level * ROWS, (level + 1) * ROWS)
                    cols = slice(quarter * COLS, (quarter + 1) * COLS)
                    ahi[rows, cols] = high
                    alo[rows, cols] = low
            along_lon()
            for level in range(LEVELS):
                for t in range(TILES):
                    work[t, level_rows(level), :] = mixed[t, level * ROWS : (level + 1) * ROWS, :]

        def update(r, carry):
            rows = pl.ds(pl.multiple_of(r * LEVELS, LEVELS), LEVELS)
            applied = jnp.concatenate([work[t, rows, :] for t in range(TILES)], axis=1)
            out[w, r] = field[w, r + STEPS] - 0.5 * applied
            return carry

        lax.fori_loop(0, ROWS, update, 0, unroll=2)

    ends_copy = pltpu.make_async_remote_copy(
        src_ref=ends, dst_ref=arrived, send_sem=es_sem, recv_sem=er_sem,
        device_id=(sibling, lat), device_id_type=MESH,
    )

    loads[0].wait()

    @pl.when(core == 0)
    def _():
        def copy_row(r, carry):
            put_row(r, field[0, r + STEPS])
            return carry

        lax.fori_loop(0, ROWS, copy_row, 0, unroll=2)
        send_forward(0, work)

    loads[3].wait()
    interior(3, 0, to_ends)
    loads[1].wait()
    interior(0, 1, to_defect(1), hand_over)
    landed(10, 11, 6, 7, 0, 1)
    window_halo(1)
    edges(3, 0, to_ends)

    @pl.when(core == 0)
    def _():
        ends_copy.start()

    edges(0, 1, to_defect(1))
    send_forward(1, work)
    window_halo(2)

    @pl.when(core == 1)
    def _():
        ends_copy.wait_recv()

        def first_defect(r, carry):
            rows = pl.ds(pl.multiple_of(r * LEVELS, LEVELS), LEVELS)
            before = jnp.concatenate([arrived[t, rows, :] for t in range(TILES)], axis=1)
            put_row(r, field[0, r + STEPS] - before)
            return carry

        lax.fori_loop(0, ROWS, first_defect, 0, unroll=2)
        send_forward(0, work)

    @pl.when(win == 1)
    def _():
        send_end_state()

    split_into(0, rhi, rlo)
    factor_loads[1].start()
    loads[2].wait()
    integrate(1, to_defect(2))
    split_work()
    along_lon()
    send_forward(2, mixed)

    integrate(2, to_defect(3))
    split_work()
    along_lon()
    send_forward(3, mixed)
    split_into(1, lhi, llo)
    mix(1, hold=True)

    forward_sent(1)
    forward_sent(2)
    send_back(1)
    mix(2, hold=True)
    forward_sent(0)
    send_back(2)

    @pl.when(win == 0)
    def _():
        pltpu.make_async_copy(recv_more, recv_more, mr_sem).wait()
        pltpu.make_async_copy(recv.at[0], recv.at[0], fr_sem.at[0]).wait()

        def subtract(k, carry):
            rows = pl.ds(pl.multiple_of(k * 64, 64), 64)
            recv[0, rows, :] = recv[0, rows, :] - recv_more[rows, :]
            return carry

        lax.fori_loop(0, NLAT // 64, subtract, 0)

    @pl.when(win != 0)
    def _():
        pltpu.make_async_copy(recv.at[0], recv.at[0], fr_sem.at[0]).wait()

    mix(0, hold=True, here=True)

    mix(3, hold=True)
    rows_sent(1)
    send_back(0)
    finish_window(1, False)
    rows_sent(2)
    send_back(3)
    finish_window(2, True)
    finish_window(0, False)
    finish_window(3, True)
    rows_sent(0)
    rows_sent(3)
    forward_sent(3)

    for copy in halos.values():
        copy.wait_send()

    @pl.when(core == 0)
    def _():
        ends_copy.wait_send()

    @pl.when(win == 1)
    def _():
        pltpu.make_async_copy(send_more, send_more, ms_sem).wait()


def shards(increments, courant_lon, courant_lat, lat_factor, lon_factor):
    any_space = pl.BlockSpec(memory_space=pl.ANY)
    strip = (EXT, LEVELS, NLON)
    dma = pltpu.SemaphoreType.DMA
    return pl.pallas_call(
        kernel,
        out_shape=pltpu.VMEM((WINS, ROWS, LEVELS, NLON), f32),
        in_specs=[any_space] * 5,
        out_specs=pl.BlockSpec(memory_space=pltpu.VMEM),
        scratch_shapes=[
            pltpu.VMEM((WINS,) + strip, f32),
            pltpu.VMEM((2,) + strip, f32),
            pltpu.VMEM((EXT, LEVELS, 128), f32),
            pltpu.VMEM((EXT, LEVELS, 128), f32),
            pltpu.VMEM((2,) + strip, f32),
            pltpu.VMEM((2,) + strip, f32),
            pltpu.VMEM((NLAT, NLON), f32),
            pltpu.VMEM((NLAT, NLAT), bf16),
            pltpu.VMEM((NLAT, NLAT), bf16),
            pltpu.VMEM((NLON, NLON), bf16),
            pltpu.VMEM((NLON, NLON), bf16),
            pltpu.VMEM((TILES, ROWS * LEVELS, 128), f32),
            pltpu.VMEM((TILES, ROWS * LEVELS, 128), f32),
            pltpu.VMEM((TILES, ROWS * LEVELS, 128), f32),
            pltpu.VMEM((TILES, ROWS * LEVELS, 128), f32),
            pltpu.VMEM((ROWS * LEVELS, NLON), bf16),
            pltpu.VMEM((ROWS * LEVELS, NLON), bf16),
            pltpu.VMEM((NLAT, COLS), bf16),
            pltpu.VMEM((NLAT, COLS), bf16),
            pltpu.VMEM((WINS, LATS, ROWS, COLS), f32),
            pltpu.VMEM((WINS, NLAT, COLS), f32),
            pltpu.VMEM((WINS, NLAT, COLS), f32),
            pltpu.VMEM((WINS, LATS, ROWS, COLS), f32),
            pltpu.VMEM((LATS, ROWS, COLS), f32),
            pltpu.VMEM((NLAT, COLS), f32),
            dma((6,)),
            dma((2,)),
            dma((12,)),
            dma((12,)),
            dma,
            dma,
            dma((WINS,)),
            dma((WINS,)),
            dma((WINS,)),
            dma((WINS,)),
            dma,
            dma,
        ],
        compiler_params=pltpu.CompilerParams(
            collective_id=0, has_side_effects=True, vmem_limit_bytes=56 << 20
        ),
        name="subwindows",
    )(increments, courant_lon, courant_lat, lat_factor, lon_factor)


def solution(mesh):
    in_specs = (P("win", "lat", None, None), P("lat", None, None), P("lat", None, None), P(), P())
    out_specs = P("win", "lat", None, None)
    return jax.shard_map(shards, mesh=mesh, in_specs=in_specs, out_specs=out_specs, check_vma=False)
```

```python
import math

import jax
import jax.numpy as jnp
from jax import lax
from jax.experimental import pallas as pl
from jax.experimental.pallas import tpu as pltpu
from jax.sharding import PartitionSpec as P

STEPS = 4
WINS = 4
ROWS = 32
LEVELS = 8
NLON = 1024
NLAT = 1024
LATS = 32
EXT = ROWS + 2 * STEPS
COLS = 256
TILES = NLON // 128
UNROLL = 2
MESH = pl.DeviceIdType.MESH

diffusion = 0.125
turning_scale = 0.6

f32 = jnp.float32
bf16 = jnp.bfloat16


def split(value):
    high = value.astype(bf16)
    low = (value - high.astype(f32)).astype(bf16)
    return high, low


def dot(a, b):
    return jnp.dot(a, b, preferred_element_type=f32)


def kernel(
    inc, clon, clat, lat_fac, lon_fac,
    out,
    field, co, cos_t, sin_t, odd_steps, even_steps,
    stage, lhi, llo, rhi, rlo,
    ends, arrived, work, mixed, ahi, alo, xhi, xlo,
    send, recv, back, ret, send_more, recv_more,
    load_sem, stage_sem, hs_sem, hr_sem, es_sem, er_sem,
    fs_sem, fr_sem, bs_sem, br_sem, ms_sem, mr_sem,
):
    lat = lax.axis_index("lat")
    win = lax.axis_index("win")
    other = lax.rem(win + 2, 4)
    north = lax.rem(lat + LATS - 1, LATS)
    south = lax.rem(lat + 1, LATS)
    core = lax.rem(win, 2)
    sibling = win + 1 - 2 * core

    loads = []
    for w in range(WINS):
        loads.append(
            pltpu.make_async_copy(inc.at[w], field.at[w, pl.ds(STEPS, ROWS)], load_sem.at[w])
        )
    loads.append(pltpu.make_async_copy(clon, co.at[0, pl.ds(STEPS, ROWS)], load_sem.at[4]))
    loads.append(pltpu.make_async_copy(clat, co.at[1, pl.ds(STEPS, ROWS)], load_sem.at[5]))
    for copy in (loads[4], loads[5], loads[0], loads[3], loads[1], loads[2]):
        copy.start()
    factor_loads = [
        pltpu.make_async_copy(lon_fac, stage, stage_sem.at[0]),
        pltpu.make_async_copy(lat_fac, stage, stage_sem.at[1]),
    ]
    factor_loads[0].start()

    barrier = pltpu.get_barrier_semaphore()

    def greet(k, carry):
        pl.semaphore_signal(
            barrier, inc=1, device_id=(other, lax.rem(lat + k, LATS)), device_id_type=MESH
        )
        return carry

    for where in ((win, north), (win, south), (sibling, lat)):
        pl.semaphore_signal(barrier, inc=1, device_id=where, device_id_type=MESH)
    lax.fori_loop(0, LATS, greet, 0)

    def greet_more(k, carry):
        pl.semaphore_signal(
            barrier, inc=1, device_id=(1, lax.rem(lat + k, LATS)), device_id_type=MESH
        )
        return carry

    @pl.when(win == 0)
    def _():
        lax.fori_loop(0, LATS, greet_more, 0)

    row = lax.broadcasted_iota(jnp.int32, (EXT, LEVELS, 128), 0) + (lat * ROWS - STEPS)
    inside = ((row >= 0) & (row < NLAT)).astype(f32)
    theta = turning_scale * jnp.cos(math.pi * (row.astype(f32) + 0.5) / NLAT)
    even3 = lax.rem(lax.broadcasted_iota(jnp.int32, (EXT, LEVELS, 128), 1), 2) == 0
    cos_t[...] = 0.5 * jnp.cos(theta) * inside
    sin_half = 0.5 * jnp.sin(theta) * inside
    sin_t[...] = jnp.where(even3, sin_half, -sin_half)

    def coefficients(r, carry):
        co[0, r] = 0.25 - co[0, r]
        co[1, r] = 0.25 - co[1, r]
        return carry

    loads[4].wait()
    loads[5].wait()
    lax.fori_loop(STEPS, STEPS + ROWS, coefficients, 0, unroll=2)

    @pl.when(win == 1)
    def _():
        pl.semaphore_wait(barrier, 2 * LATS + 3)

    @pl.when(win != 1)
    def _():
        pl.semaphore_wait(barrier, LATS + 3)

    halos = {}

    def courant_group(wraps):
        return jnp.where(wraps, other, win)

    def halo(src, dst, slot, where, group=None):
        copy = pltpu.make_async_remote_copy(
            src_ref=src, dst_ref=dst, send_sem=hs_sem.at[slot], recv_sem=hr_sem.at[slot],
            device_id=(win if group is None else group, where), device_id_type=MESH,
        )
        copy.start()
        halos[slot] = copy

    def window_halo(w):
        halo(inc.at[w, pl.ds(ROWS - STEPS, STEPS)], field.at[w, pl.ds(0, STEPS)], 2 * w, south)
        halo(inc.at[w, pl.ds(0, STEPS)], field.at[w, pl.ds(STEPS + ROWS, STEPS)], 2 * w + 1, north)

    def landed(*slots):
        for slot in slots:
            halos[slot].wait_recv()

    EDGE = STEPS - 1
    top = pl.ds(1, EDGE)
    bottom = pl.ds(STEPS + ROWS, EDGE)
    window_halo(3)
    halo(co.at[core, pl.ds(STEPS + ROWS - EDGE, EDGE)], co.at[core, top], 8, south,
         courant_group(lax.rem(lat, 4) == 3))
    halo(co.at[core, pl.ds(STEPS, EDGE)], co.at[core, bottom], 9, north,
         courant_group(lax.rem(lat, 4) == 0))
    window_halo(0)

    def hand_over():
        landed(8, 9)
        halo(co.at[core, top], co.at[core, top], 10, lat, sibling)
        halo(co.at[core, bottom], co.at[core, bottom], 11, lat, sibling)

    def split_into(slot, high_ref, low_ref):
        def some(k, carry):
            rows = pl.ds(pl.multiple_of(k * 32, 32), 32)
            high, low = split(stage[rows, :])
            high_ref[rows, :] = high
            low_ref[rows, :] = low
            return carry

        factor_loads[slot].wait()
        lax.fori_loop(0, NLAT // 32, some, 0)

    even = lax.rem(lax.broadcasted_iota(jnp.int32, (LEVELS, NLON), 0), 2) == 0

    def two_rows(src, r):
        near = [src[r - 1], src[r], src[r + 1], src[r + 2]]
        done = []
        for i in range(2):
            n, c, s = near[i : i + 3]
            e = pltpu.roll(c, NLON - 1, 1)
            w = pltpu.roll(c, 1, 1)
            y = (c + 0.5 * (w + n)) + co[0, r + i] * (e - w) + co[1, r + i] * (s - n)
            swapped = jnp.where(even, pltpu.roll(y, LEVELS - 1, 0), pltpu.roll(y, 1, 0))
            cosine = jnp.concatenate([cos_t[r + i]] * TILES, axis=1)
            sine = jnp.concatenate([sin_t[r + i]] * TILES, axis=1)
            done.append(cosine * y + sine * swapped)
        return done

    def advance(src, dst, first, last):
        def rows(k, carry):
            r = first + 2 * k
            dst[r], dst[r + 1] = two_rows(src, r)
            return carry

        lax.fori_loop(0, (last - first) // 2, rows, 0, unroll=UNROLL)

    def last_step(src, first, last, finish):
        def some(k, carry):
            r = first + 2 * k
            one, two = two_rows(src, r + STEPS)
            finish(r, one)
            finish(r + 1, two)
            return carry

        lax.fori_loop(0, (last - first) // 2, some, 0, unroll=UNROLL)

    def outside_is_zero(w):
        @pl.when(lat == 0)
        def _():
            field[w, 0:STEPS] = jnp.zeros((STEPS, LEVELS, NLON), f32)

        @pl.when(lat == LATS - 1)
        def _():
            field[w, STEPS + ROWS : EXT] = jnp.zeros((STEPS, LEVELS, NLON), f32)

    def stages(w, half):
        t1, t2 = odd_steps.at[half], even_steps.at[half]
        return (field.at[w], t1, 1), (t1, t2, 2), (t2, t1, 3)

    def integrate(w, finish):
        landed(2 * w, 2 * w + 1)
        outside_is_zero(w)
        for src, dst, step in stages(w, 0):
            advance(src, dst, step, EXT - step)
        last_step(odd_steps.at[0], 0, ROWS, finish)

    def interior(w, half, finish, between=None):
        for src, dst, step in stages(w, half):
            advance(src, dst, STEPS + step, EXT - STEPS - step)
            if step == 2 and between is not None:
                between()
        last_step(odd_steps.at[half], STEPS, ROWS - STEPS, finish)

    def edges(w, half, finish):
        outside_is_zero(w)
        for src, dst, step in stages(w, half):
            advance(src, dst, step, step + STEPS)
            advance(src, dst, EXT - step - STEPS, EXT - step)
        last_step(odd_steps.at[half], 0, STEPS, finish)
        last_step(odd_steps.at[half], ROWS - STEPS, ROWS, finish)

    def put_row(r, value, target=None):
        target = work if target is None else target
        for t in range(TILES):
            target[t, pl.ds(pl.multiple_of(r * LEVELS, LEVELS), LEVELS), :] = value[
                :, t * 128 : (t + 1) * 128
            ]

    def level_rows(level):
        return pl.ds(level, ROWS, stride=LEVELS)

    def to_defect(w):
        def finish(r, value):
            put_row(r, field[w, r + STEPS] - value)

        return finish

    def to_ends(r, value):
        put_row(r, value, ends)

    def along_lon():
        def block(k, carry):
            cols = pl.ds(pl.multiple_of(k * 256, 256), 256)
            right = rhi[:, cols]
            both = dot(ahi[...], right) + dot(alo[...], right) + dot(ahi[...], rlo[:, cols])
            mixed[2 * k] = both[:, :128]
            mixed[2 * k + 1] = both[:, 128:]
            return carry

        lax.fori_loop(0, NLON // 256, block, 0)

    def split_work():
        for t in range(TILES):
            high, low = split(work[t])
            ahi[:, t * 128 : (t + 1) * 128] = high
            alo[:, t * 128 : (t + 1) * 128] = low

    def by_level(source, target):
        for level in range(LEVELS):
            for t in range(TILES):
                target[level * 4 + t // 2, :, (t % 2) * 128 : (t % 2 + 1) * 128] = source[
                    t, level_rows(level), :
                ]

    def send_end_state():
        by_level(ends, send_more)

        def go(k, carry):
            j = lax.rem(lat + k, LATS)
            pltpu.make_async_remote_copy(
                src_ref=send_more.at[j],
                dst_ref=recv_more.at[pl.ds(pl.multiple_of(lat * ROWS, ROWS), ROWS)],
                send_sem=ms_sem, recv_sem=mr_sem,
                device_id=(0, j), device_id_type=MESH,
            ).start()
            return carry

        lax.fori_loop(0, LATS, go, 0)

    def send_forward(w, source):
        by_level(source, send.at[w])

        def go(k, carry):
            j = lax.rem(lat + k, LATS)
            pltpu.make_async_remote_copy(
                src_ref=send.at[w, j],
                dst_ref=recv.at[w, pl.ds(pl.multiple_of(lat * ROWS, ROWS), ROWS)],
                send_sem=fs_sem.at[w], recv_sem=fr_sem.at[w],
                device_id=(other, j), device_id_type=MESH,
            ).start()
            return carry

        lax.fori_loop(0, LATS, go, 0)

    def mix(w, hold=False, here=False):
        if not here:
            pltpu.make_async_copy(recv.at[w], recv.at[w], fr_sem.at[w]).wait()

        def some(k, carry):
            rows = pl.ds(pl.multiple_of(k * 128, 128), 128)
            high, low = split(recv[w, rows, :])
            xhi[rows, :] = high
            xlo[rows, :] = low
            return carry

        lax.fori_loop(0, NLAT // 128, some, 0)

        def block(k, carry):
            first = lax.rem(lat // 8 + k, 4)
            rows = pl.ds(pl.multiple_of(first * 256, 256), 256)
            left = lhi[rows, :]
            back[w, rows, :] = (
                dot(left, xhi[...]) + dot(left, xlo[...]) + dot(llo[rows, :], xhi[...])
            )

            def go(i, inner):
                j = first * 8 + lax.rem(lat + i, 8)
                pltpu.make_async_remote_copy(
                    src_ref=back.at[w, pl.ds(pl.multiple_of(j * ROWS, ROWS), ROWS)],
                    dst_ref=ret.at[w, lat],
                    send_sem=bs_sem.at[w], recv_sem=br_sem.at[w],
                    device_id=(other, j), device_id_type=MESH,
                ).start()
                return inner

            if not hold:
                lax.fori_loop(0, 8, go, 0)
            return carry

        lax.fori_loop(0, 4, block, 0)

    def send_back(w):
        def go(k, carry):
            j = lax.rem(lat + k, LATS)
            pltpu.make_async_remote_copy(
                src_ref=back.at[w, pl.ds(pl.multiple_of(j * ROWS, ROWS), ROWS)],
                dst_ref=ret.at[w, lat],
                send_sem=bs_sem.at[w], recv_sem=br_sem.at[w],
                device_id=(other, j), device_id_type=MESH,
            ).start()
            return carry

        lax.fori_loop(0, LATS, go, 0)

    def rows_sent(w):
        pltpu.make_async_copy(back.at[w], back.at[w], bs_sem.at[w]).wait()

    def forward_sent(w):
        pltpu.make_async_copy(send.at[w], send.at[w], fs_sem.at[w]).wait()

    def finish_window(w, lon_done):
        pltpu.make_async_copy(ret.at[w], ret.at[w], br_sem.at[w]).wait()
        if lon_done:
            for level in range(LEVELS):
                for t in range(TILES):
                    work[t, level_rows(level), :] = ret[
                        w, level * 4 + t // 2, :, (t % 2) * 128 : (t % 2 + 1) * 128
                    ]
        else:
            for level in range(LEVELS):
                for quarter in range(4):
                    high, low = split(ret[w, level * 4 + quarter])
                    rows = slice(level * ROWS, (level + 1) * ROWS)
                    cols = slice(quarter * COLS, (quarter + 1) * COLS)
                    ahi[rows, cols] = high
                    alo[rows, cols] = low
            along_lon()
            for level in range(LEVELS):
                for t in range(TILES):
                    work[t, level_rows(level), :] = mixed[t, level * ROWS : (level + 1) * ROWS, :]

        def update(r, carry):
            rows = pl.ds(pl.multiple_of(r * LEVELS, LEVELS), LEVELS)
            applied = jnp.concatenate([work[t, rows, :] for t in range(TILES)], axis=1)
            out[w, r] = field[w, r + STEPS] - 0.5 * applied
            return carry

        lax.fori_loop(0, ROWS, update, 0, unroll=2)

    ends_copy = pltpu.make_async_remote_copy(
        src_ref=ends, dst_ref=arrived, send_sem=es_sem, recv_sem=er_sem,
        device_id=(sibling, lat), device_id_type=MESH,
    )

    loads[0].wait()

    @pl.when(core == 0)
    def _():
        def copy_row(r, carry):
            put_row(r, field[0, r + STEPS])
            return carry

        lax.fori_loop(0, ROWS, copy_row, 0, unroll=2)
        send_forward(0, work)

    loads[3].wait()
    interior(3, 0, to_ends)
    loads[1].wait()
    interior(0, 1, to_defect(1), hand_over)
    landed(10, 11, 6, 7, 0, 1)
    window_halo(1)
    window_halo(2)
    edges(3, 0, to_ends)

    @pl.when(core == 0)
    def _():
        ends_copy.start()

    edges(0, 1, to_defect(1))
    send_forward(1, work)

    @pl.when(core == 1)
    def _():
        ends_copy.wait_recv()

        def first_defect(r, carry):
            rows = pl.ds(pl.multiple_of(r * LEVELS, LEVELS), LEVELS)
            before = jnp.concatenate([arrived[t, rows, :] for t in range(TILES)], axis=1)
            put_row(r, field[0, r + STEPS] - before)
            return carry

        lax.fori_loop(0, ROWS, first_defect, 0, unroll=2)
        send_forward(0, work)

    @pl.when(win == 1)
    def _():
        send_end_state()

    split_into(0, rhi, rlo)
    factor_loads[1].start()
    loads[2].wait()
    integrate(1, to_defect(2))
    split_work()
    along_lon()
    send_forward(2, mixed)

    integrate(2, to_defect(3))
    split_work()
    along_lon()
    send_forward(3, mixed)
    split_into(1, lhi, llo)
    mix(1, hold=True)

    forward_sent(1)
    forward_sent(2)
    send_back(1)
    mix(2, hold=True)
    forward_sent(0)
    send_back(2)

    @pl.when(win == 0)
    def _():
        pltpu.make_async_copy(recv_more, recv_more, mr_sem).wait()
        pltpu.make_async_copy(recv.at[0], recv.at[0], fr_sem.at[0]).wait()

        def subtract(k, carry):
            rows = pl.ds(pl.multiple_of(k * 64, 64), 64)
            recv[0, rows, :] = recv[0, rows, :] - recv_more[rows, :]
            return carry

        lax.fori_loop(0, NLAT // 64, subtract, 0)

    @pl.when(win != 0)
    def _():
        pltpu.make_async_copy(recv.at[0], recv.at[0], fr_sem.at[0]).wait()

    mix(0, hold=True, here=True)

    forward_sent(3)
    send_back(0)
    mix(3, hold=True)
    rows_sent(1)
    send_back(3)
    finish_window(1, False)
    rows_sent(2)
    finish_window(2, True)
    finish_window(0, False)
    finish_window(3, True)
    rows_sent(0)
    rows_sent(3)

    for copy in halos.values():
        copy.wait_send()

    @pl.when(core == 0)
    def _():
        ends_copy.wait_send()

    @pl.when(win == 1)
    def _():
        pltpu.make_async_copy(send_more, send_more, ms_sem).wait()


def shards(increments, courant_lon, courant_lat, lat_factor, lon_factor):
    any_space = pl.BlockSpec(memory_space=pl.ANY)
    strip = (EXT, LEVELS, NLON)
    dma = pltpu.SemaphoreType.DMA
    return pl.pallas_call(
        kernel,
        out_shape=pltpu.VMEM((WINS, ROWS, LEVELS, NLON), f32),
        in_specs=[any_space] * 5,
        out_specs=pl.BlockSpec(memory_space=pltpu.VMEM),
        scratch_shapes=[
            pltpu.VMEM((WINS,) + strip, f32),
            pltpu.VMEM((2,) + strip, f32),
            pltpu.VMEM((EXT, LEVELS, 128), f32),
            pltpu.VMEM((EXT, LEVELS, 128), f32),
            pltpu.VMEM((2,) + strip, f32),
            pltpu.VMEM((2,) + strip, f32),
            pltpu.VMEM((NLAT, NLON), f32),
            pltpu.VMEM((NLAT, NLAT), bf16),
            pltpu.VMEM((NLAT, NLAT), bf16),
            pltpu.VMEM((NLON, NLON), bf16),
            pltpu.VMEM((NLON, NLON), bf16),
            pltpu.VMEM((TILES, ROWS * LEVELS, 128), f32),
            pltpu.VMEM((TILES, ROWS * LEVELS, 128), f32),
            pltpu.VMEM((TILES, ROWS * LEVELS, 128), f32),
            pltpu.VMEM((TILES, ROWS * LEVELS, 128), f32),
            pltpu.VMEM((ROWS * LEVELS, NLON), bf16),
            pltpu.VMEM((ROWS * LEVELS, NLON), bf16),
            pltpu.VMEM((NLAT, COLS), bf16),
            pltpu.VMEM((NLAT, COLS), bf16),
            pltpu.VMEM((WINS, LATS, ROWS, COLS), f32),
            pltpu.VMEM((WINS, NLAT, COLS), f32),
            pltpu.VMEM((WINS, NLAT, COLS), f32),
            pltpu.VMEM((WINS, LATS, ROWS, COLS), f32),
            pltpu.VMEM((LATS, ROWS, COLS), f32),
            pltpu.VMEM((NLAT, COLS), f32),
            dma((6,)),
            dma((2,)),
            dma((12,)),
            dma((12,)),
            dma,
            dma,
            dma((WINS,)),
            dma((WINS,)),
            dma((WINS,)),
            dma((WINS,)),
            dma,
            dma,
        ],
        compiler_params=pltpu.CompilerParams(
            collective_id=0, has_side_effects=True, vmem_limit_bytes=56 << 20
        ),
        name="subwindows",
    )(increments, courant_lon, courant_lat, lat_factor, lon_factor)


def solution(mesh):
    in_specs = (P("win", "lat", None, None), P("lat", None, None), P("lat", None, None), P(), P())
    out_specs = P("win", "lat", None, None)
    return jax.shard_map(shards, mesh=mesh, in_specs=in_specs, out_specs=out_specs, check_vma=False)
```
